1024 devices in a mesh: row: 64 (over z, x), col: 16 (over y, core).
Axes of the slice: x: 4, y: 8, z: 16, core: 2. Of those that a mesh axis runs over, the one named last changes fastest.
Arguments:
- activations: bfloat16 [2048, 12288], P('col', 'row'), may hold values from -6 to 6
- weight_tiles: bfloat16 [16, 64, 12, 4096], P('col', 'row'), may hold values from -0.125 to 0.125
- tile_ids: int32 [16, 64, 12], P('col', 'row'), may hold values from 0 to 71, as said below
- tile_counts: int32 [16, 64], P('col', 'row'), may hold values from 7 to 12, as said below
- upstream: bfloat16 [2048, 24576], P('col', 'row'), may hold values from -0.119628906 to 0.119628906
Outputs:
- output: bfloat16 [2048, 24576], P('col', 'row')
- weight_grad: bfloat16 [16, 64, 12, 4096], P('col', 'row')
The draws below stay inside these ranges and needn't reach their ends.
Inputs may be any that keep to these rules, and one draw needn't show every extreme that they name: `tile_ids`: within one block the 12 slots name distinct tiles; only slots below the block's count are used. `tile_counts`: some block is full in every draw.
All inputs are finite; a program needn't handle non-finite values.
Results may differ from the reference program's by a relative error of at most 0.017.
Values may be sent and summed in bfloat16 or wider, within the bound.
No kernel may reach another device: no remote copies, remote signals or barrier semaphores. Data moves between devices by JAX's collectives and lax.ppermute only.
A program may use at most 32 MiB of HBM per device.

```python
import jax
import jax.numpy as jnp
from jax import lax

D = 12288
FF = 24576
TILE = 64
CAP = 12
TOK_DEV = 128
TOK = 2048
TPB = 72
N_ROW = 64
N_COL = 16


def pick_tiles(block_key):
    return jax.random.permutation(block_key, TPB)[:CAP]


def draw_tile_ids(key, part):
    keys = jax.random.split(key, N_COL * N_ROW)
    chosen = jax.vmap(pick_tiles)(keys)
    return chosen.reshape(N_COL, N_ROW, CAP).astype(jnp.int32)


def draw_tile_counts(key, part):
    counts = jax.random.randint(key, (N_COL * N_ROW,), CAP // 2 + 1, CAP + 1)
    place = jax.random.randint(jax.random.fold_in(key, 7), (), 0, N_COL * N_ROW)
    counts = jnp.where(jnp.arange(N_COL * N_ROW) == place, CAP, counts)
    return counts.reshape(N_COL, N_ROW).astype(jnp.int32)


def steps_of(rng, shape, pieces, least, largest):
    factor_of, own = 1.0, jax.random.fold_in(rng, 6)
    for dim, blocks in pieces:
        draws = jnp.exp(jax.random.uniform(jax.random.fold_in(own, dim), (blocks,), jnp.float32, least / len(pieces), largest / len(pieces)))
        factor_of = factor_of * jnp.repeat(draws, shape[dim] // blocks).reshape([-1 if axis == dim else 1 for axis in range(len(shape))])
    return factor_of


def gaussian(stream_key, dims, spread, bound, pieces=(), kind=jnp.bfloat16):
    entries = spread * jax.random.normal(stream_key, dims, jnp.float32)
    if pieces:
        entries = entries * steps_of(stream_key, dims, pieces, -0.22, 0.18)
    return jnp.clip(entries, -bound, bound).astype(kind)


def setup_inputs(seed: int = 0) -> dict:
    streams_of = jax.random.split(jax.random.key(seed), 6)
    activations = gaussian(streams_of[0], (TOK, D), 1.0, 6.0, ((0, 16), (1, 64)))
    weight_tiles = gaussian(streams_of[1], (N_COL, N_ROW, CAP, TILE * TILE), (D // 5) ** -0.5, 0.125, ((0, 16), (1, 64)))
    tile_ids = draw_tile_ids(jax.random.fold_in(streams_of[5], 71), 0)
    tile_counts = draw_tile_counts(jax.random.fold_in(streams_of[5], 71), 0)
    upstream = gaussian(streams_of[4], (TOK, FF), 0.02, 0.119628906, ((0, 16), (1, 64)))
    return dict(activations=activations, weight_tiles=weight_tiles, tile_ids=tile_ids, tile_counts=tile_counts, upstream=upstream)


def gelu_parts(pre):
    cumul = 0.5 * (1.0 + jax.scipy.special.erf(pre * 0.7071067811865476))
    density = jnp.exp(-0.5 * pre * pre) * 0.3989422804014327
    return cumul, density


def reference(activations, weight_tiles, tile_ids, tile_counts, upstream):
    d_block = D // N_COL // TILE
    per_col = FF // N_ROW // TILE
    ff_local = FF // N_ROW
    slots = N_COL * CAP
    x_all = activations.reshape(TOK, D // TILE, TILE)
    owner = jnp.arange(slots, dtype=jnp.int32) // CAP
    position = jnp.arange(slots, dtype=jnp.int32) % CAP

    def one_block(index):
        tiles = lax.dynamic_index_in_dim(weight_tiles, index, 1, keepdims=False)
        tiles = tiles.reshape(slots, TILE, TILE).astype(jnp.float32)
        slot_ids = lax.dynamic_index_in_dim(tile_ids, index, 1, keepdims=False).reshape(slots).astype(jnp.int32)
        counts_col = lax.dynamic_index_in_dim(tile_counts, index, 1, keepdims=False).astype(jnp.int32)
        live = position < counts_col[owner]
        d_tile = (owner * d_block + slot_ids // per_col).astype(jnp.int32)
        f_tile = (slot_ids % per_col).astype(jnp.int32)
        placing = ((f_tile[:, None] == jnp.arange(per_col, dtype=jnp.int32)[None, :]) & live[:, None]).astype(jnp.float32)
        x_tiles = jnp.take(x_all, d_tile, axis=1).astype(jnp.float32)
        partial_value = jnp.einsum("tsk,skn->tsn", x_tiles, tiles)
        pre = jnp.einsum("tsn,sf->tfn", partial_value, placing, precision=lax.Precision.HIGHEST).reshape(TOK, ff_local)
        cumul, density = gelu_parts(pre)
        output = (pre * cumul).astype(jnp.bfloat16)
        up_block = lax.dynamic_slice_in_dim(upstream, index * ff_local, ff_local, 1).astype(jnp.float32)
        grad_pre = (up_block * (cumul + pre * density)).astype(jnp.bfloat16)
        g_tiles = jnp.take(grad_pre.reshape(TOK, per_col, TILE), f_tile, axis=1).astype(jnp.float32)
        groups = jnp.einsum("gtsk,gtsn->gskn", x_tiles.reshape(N_COL, TOK_DEV, slots, TILE), g_tiles.reshape(N_COL, TOK_DEV, slots, TILE))
        rounded = lax.optimization_barrier(groups.astype(jnp.bfloat16)).astype(jnp.float32)
        summed = jnp.sum(rounded, axis=0).reshape(N_COL, CAP, TILE * TILE)
        grad = jnp.where(live.reshape(N_COL, CAP)[:, :, None], summed, 0.0).astype(jnp.bfloat16)
        return output, grad

    outputs, grads = lax.map(one_block, jnp.arange(N_ROW, dtype=jnp.int32))
    output = jnp.transpose(outputs, (1, 0, 2)).reshape(TOK, FF)
    weight_grad = jnp.transpose(grads, (1, 0, 2, 3))
    return (output, weight_grad)
```

```python
import jax
import jax.numpy as jnp
from jax import lax
from jax.experimental import pallas as pl
from jax.experimental.pallas import tpu as pltpu
from jax.sharding import Mesh, PartitionSpec as P

TILE = 64
CAP = 12
PAIRS = CAP // 2
PACK = PAIRS * TILE
META = 16
ROWS = PACK + META
PER_COL = 6
SUB = 3
NZ, NX, NY = 16, 4, 8
SHARD = 192
FF_LOC = 384
TOK = 128


def slot_info(meta, row, slot):
    tid = meta[row, slot]
    d = tid // PER_COL
    return d, tid - d * PER_COL


def kernel(meta, here, x0, x1, x3, x2a, x2b, w0, w1, up, out, dw, xs, ws, acc, res, sem):
    my_x, my_core = here[0], here[1]
    half = NZ // 2
    copies = [
        pltpu.make_async_copy(x0, xs.at[0], sem.at[0]),
        pltpu.make_async_copy(x1, xs.at[1], sem.at[1]),
        pltpu.make_async_copy(x2a, xs.at[2, 0 : half * SHARD], sem.at[2]),
        pltpu.make_async_copy(x2b, xs.at[2, half * SHARD : NZ * SHARD], sem.at[3]),
        pltpu.make_async_copy(x3, xs.at[3], sem.at[4]),
    ]
    for c in copies:
        c.start()
    lane = lax.broadcasted_iota(jnp.int32, (1, 2 * TILE), 1)
    acc[...] = jnp.zeros_like(acc)
    for c in copies:
        c.wait()

    def x_rows(row, z):
        parts = []
        for s in range(CAP):
            d, _ = slot_info(meta, row, s)
            xc = d // SUB
            q = (xc - my_x + NX) % NX
            start = pl.multiple_of(z * SHARD + (d - xc * SUB) * TILE, TILE)
            parts.append(xs[q, pl.ds(start, TILE), :])
        return jnp.concatenate(parts, axis=0)

    for rc in range(2):
        wref = w0 if rc == 0 else w1
        core = my_core if rc == 0 else 1 - my_core

        def forward(y, carry, rc=rc, wref=wref, core=core):
            row = rc * NY + y
            count = meta[row, CAP]
            ws[...] = jnp.zeros_like(ws)
            for m in range(PAIRS):
                _, f0 = slot_info(meta, row, 2 * m)
                _, f1 = slot_info(meta, row, 2 * m + 1)
                tile = wref[y, m * TILE : (m + 1) * TILE, :]
                lo = jnp.where((lane < TILE) & (2 * m < count), 1.0, 0.0).astype(jnp.bfloat16)
                hi = jnp.where((lane >= TILE) & (2 * m + 1 < count), 1.0, 0.0).astype(jnp.bfloat16)
                cols = slice(m * 2 * TILE, (m + 1) * 2 * TILE)
                ws[pl.ds(pl.multiple_of(f0 * TILE, TILE), TILE), cols] = tile * lo
                second = pl.ds(pl.multiple_of(f1 * TILE, TILE), TILE)
                ws[second, cols] = ws[second, cols] + tile * hi
            acc[...] += jnp.dot(ws[...], x_rows(row, 2 * y + core), preferred_element_type=jnp.float32)
            return carry

        lax.fori_loop(0, NY, forward, 0)

    pre = acc[...].T
    cumul = 0.5 * (1.0 + lax.erf(pre * 0.7071067811865476))
    density = jnp.exp(-0.5 * pre * pre) * 0.3989422804014327
    out[...] = (pre * cumul).astype(jnp.bfloat16)
    grad = (up[...].astype(jnp.float32) * (cumul + pre * density)).astype(jnp.bfloat16)

    for rc in range(2):
        core = my_core if rc == 0 else 1 - my_core

        def backward(y, carry, rc=rc, core=core):
            row = rc * NY + y
            res[...] = jnp.dot(x_rows(row, 2 * y + core), grad, preferred_element_type=jnp.float32)
            for m in range(PAIRS):
                picked = []
                for p in range(2):
                    s = 2 * m + p
                    _, f = slot_info(meta, row, s)
                    chunk = f // 2
                    wide = res[s * TILE : (s + 1) * TILE, pl.ds(pl.multiple_of(chunk * 2 * TILE, 2 * TILE), 2 * TILE)]
                    swapped = pltpu.roll(wide, TILE, 1)
                    picked.append(jnp.where(f - chunk * 2 == p, wide, swapped))
                dw[rc, y, m * TILE : (m + 1) * TILE, :] = jnp.where(lane < TILE, picked[0], picked[1]).astype(jnp.bfloat16)
            return carry

        lax.fori_loop(0, NY, backward, 0)


def local_step(meta, here, x0, x1, x3, x2a, x2b, w0, w1, up):
    any_spec = pl.BlockSpec(memory_space=pl.ANY)
    vmem = pl.BlockSpec(memory_space=pltpu.VMEM)
    smem = pl.BlockSpec(memory_space=pltpu.SMEM)
    return pl.pallas_call(
        kernel,
        out_shape=(
            jax.ShapeDtypeStruct((TOK, FF_LOC), jnp.bfloat16),
            jax.ShapeDtypeStruct((2, NY, PACK, 2 * TILE), jnp.bfloat16),
        ),
        in_specs=[smem, smem, any_spec, any_spec, any_spec, any_spec, any_spec, vmem, vmem, vmem],
        out_specs=(vmem, vmem),
        scratch_shapes=[
            pltpu.VMEM((NX, NZ * SHARD, TOK), jnp.bfloat16),
            pltpu.VMEM((FF_LOC, CAP * TILE), jnp.bfloat16),
            pltpu.VMEM((FF_LOC, TOK), jnp.float32),
            pltpu.VMEM((CAP * TILE, FF_LOC), jnp.float32),
            pltpu.SemaphoreType.DMA((5,)),
        ],
        cost_estimate=pl.CostEstimate(flops=5 * 10**9, bytes_accessed=8 * 10**6, transcendentals=10**5),
        name="local_step",
    )(meta, here, x0, x1, x3, x2a, x2b, w0, w1, up)


def ring(n, step):
    return [(i, (i + step) % n) for i in range(n)]


SWAP = [(0, 1), (1, 0)]


def body(activations, weight_tiles, tile_ids, tile_counts, upstream):
    packed = weight_tiles.reshape(PAIRS, 2, TILE, TILE).transpose(0, 3, 1, 2).reshape(PACK, 2 * TILE)
    meta = jnp.concatenate([tile_ids.reshape(1, CAP), tile_counts.reshape(1, 1)], axis=1)
    meta = jnp.pad(meta, ((0, META - 1), (0, 2 * TILE - CAP - 1))).astype(jnp.bfloat16)
    sent = jnp.concatenate([packed, meta], axis=0)

    wide = jnp.broadcast_to(sent[None], (NY, ROWS, 2 * TILE))
    w_own = lax.all_to_all(wide, "y", split_axis=0, concat_axis=0, tiled=True)

    x_mine = activations.T.reshape(1, SHARD // 16, 16, TOK)
    x0 = lax.all_gather(x_mine, "z", axis=0, tiled=True).reshape(NZ * SHARD, TOK)
    x3 = lax.ppermute(x0, "x", ring(NX, 1))
    x1 = lax.ppermute(x0, "x", ring(NX, -1))
    cut = NZ * SHARD // 2
    x2a = lax.ppermute(x3[:cut], "x", ring(NX, 1))
    x2b = lax.ppermute(x1[cut:], "x", ring(NX, -1))
    w_other = lax.ppermute(w_own, "core", SWAP)

    ids = jnp.concatenate([w_own[:, PACK, :], w_other[:, PACK, :]], axis=0).astype(jnp.int32)
    here = jnp.stack([lax.axis_index("x"), lax.axis_index("core")]).astype(jnp.int32)
    output, partial = local_step(ids, here, x0, x1, x3, x2a, x2b, w_own, w_other, upstream)

    arrived = lax.ppermute(partial[1], "core", SWAP)
    both = (partial[0].astype(jnp.float32) + arrived.astype(jnp.float32)).astype(jnp.bfloat16)
    parts = lax.all_to_all(both, "y", split_axis=0, concat_axis=0, tiled=True)
    summed = jnp.sum(parts.astype(jnp.float32), axis=0)
    summed = summed.reshape(PAIRS, TILE, 2, TILE).transpose(0, 2, 1, 3).reshape(CAP, TILE * TILE)
    live = jnp.arange(CAP, dtype=jnp.int32) < tile_counts.reshape(())
    grad = jnp.where(live[:, None], summed, 0.0).astype(jnp.bfloat16)
    return output, grad.reshape(1, 1, CAP, TILE * TILE)


def solution(mesh):
    fine = Mesh(mesh.devices.reshape(NZ, NX, NY, 2), ("z", "x", "y", "core"))
    rows, cols = ("z", "x"), ("y", "core")
    return jax.shard_map(
        body,
        mesh=fine,
        in_specs=(
            P(cols, rows),
            P(cols, rows, None, None),
            P(cols, rows, None),
            P(cols, rows),
            P(cols, rows),
        ),
        out_specs=(P(cols, rows), P(cols, rows, None, None)),
        check_vma=False,
    )
```

```python
import jax
import jax.numpy as jnp
from jax import lax
from jax.experimental import pallas as pl
from jax.experimental.pallas import tpu as pltpu
from jax.sharding import Mesh, PartitionSpec as P

TILE = 64
PAIR = 2 * TILE
CAP = 12
PAIRS = CAP // 2
PACK = PAIRS * TILE
META = 16
ROWS = PACK + META
PER_COL = 6
SUB = 3
F_LANE = 16
NZ, NX, NY = 16, 4, 8
SHARD = 192
X_ROWS = NX * NZ * SHARD
FF_LOC = 384
TOK = 128


VMEM = pl.BlockSpec(memory_space=pltpu.VMEM)
ANY = pl.BlockSpec(memory_space=pltpu.HBM)
SMEM = pl.BlockSpec(memory_space=pltpu.SMEM)


def aligned(start, size):
    return pl.ds(pl.multiple_of(start, size), size)


def lanes_below():
    return lax.broadcasted_iota(jnp.int32, (1, PAIR), 1) < TILE


def two(ref, start0, start1):
    return jnp.concatenate([ref[aligned(start0 * TILE, TILE), :], ref[aligned(start1 * TILE, TILE), :]], axis=0)


def slot_grads(table, b, x, grad_t, dw, y):
    low = lanes_below()
    for m in range(PAIRS):
        s = 2 * m
        cols = two(grad_t, table[b, F_LANE + s], table[b, F_LANE + s + 1])
        rows = two(x, table[b, s], table[b, s + 1])
        prod = lax.dot_general(cols, rows, (((1,), (1,)), ((), ())), preferred_element_type=jnp.float32)
        dw[y, m * TILE : (m + 1) * TILE, :] = jnp.where(low, prod[:TILE], prod[TILE:]).astype(jnp.bfloat16)


def main_kernel(table, x, w0, w1, up, out, grad_t, dw, acc, tiles0, tiles1, sem):
    copies = [pltpu.make_async_copy(w0, tiles0, sem.at[0]), pltpu.make_async_copy(w1, tiles1, sem.at[1])]
    for c in copies:
        c.start()
    acc[...] = jnp.zeros_like(acc)
    low = lanes_below()
    first = jnp.where(low, 1.0, 0.0).astype(jnp.bfloat16)
    second = jnp.where(low, 0.0, 1.0).astype(jnp.bfloat16)
    for rc, tiles in enumerate((tiles0, tiles1)):
        copies[rc].wait()

        def forward(y, carry, rc=rc, tiles=tiles):
            b = rc * NY + y
            for m in range(PAIRS):
                s = 2 * m
                tile = tiles[y, m * TILE : (m + 1) * TILE, :]
                prod = jnp.dot(
                    jnp.concatenate([tile * first, tile * second], axis=0),
                    two(x, table[b, s], table[b, s + 1]),
                    preferred_element_type=jnp.float32,
                )
                for p in range(2):
                    acc[aligned(table[b, F_LANE + s + p] * TILE, TILE), :] += prod[p * TILE : (p + 1) * TILE]
            return carry

        lax.fori_loop(0, NY, forward, 0)

    pre = acc[...].T
    cumul = 0.5 * (1.0 + lax.erf(pre * 0.7071067811865476))
    density = jnp.exp(-0.5 * pre * pre) * 0.3989422804014327
    out[...] = (pre * cumul).astype(jnp.bfloat16)
    grad_t[...] = (up[...].astype(jnp.float32) * (cumul + pre * density)).T.astype(jnp.bfloat16)

    def backward(y, carry):
        slot_grads(table, NY + y, x, grad_t, dw, y)
        return carry

    lax.fori_loop(0, NY, backward, 0)


def rest_kernel(table, x, grad_t, dw):
    def backward(y, carry):
        slot_grads(table, y, x, grad_t, dw, y)
        return carry

    lax.fori_loop(0, NY, backward, 0)


def params(mib):
    return pltpu.CompilerParams(vmem_limit_bytes=mib << 20)


def main_step(table, x, w0, w1, up):
    return pl.pallas_call(
        main_kernel,
        out_shape=(
            jax.ShapeDtypeStruct((TOK, FF_LOC), jnp.bfloat16),
            jax.ShapeDtypeStruct((FF_LOC, TOK), jnp.bfloat16),
            jax.ShapeDtypeStruct((NY, PACK, PAIR), jnp.bfloat16),
        ),
        in_specs=[SMEM, VMEM, ANY, ANY, VMEM],
        out_specs=(VMEM, VMEM, VMEM),
        scratch_shapes=[
            pltpu.VMEM((FF_LOC, TOK), jnp.float32),
            pltpu.VMEM((NY, ROWS, PAIR), jnp.bfloat16),
            pltpu.VMEM((NY, ROWS, PAIR), jnp.bfloat16),
            pltpu.SemaphoreType.DMA((2,)),
        ],
        compiler_params=params(16),
        cost_estimate=pl.CostEstimate(flops=2 * 10**9, bytes_accessed=8 * 10**6, transcendentals=10**5),
        name="main_step",
    )(table, x, w0, w1, up)


def rest_step(table, x, grad_t):
    return pl.pallas_call(
        rest_kernel,
        out_shape=jax.ShapeDtypeStruct((NY, PACK, PAIR), jnp.bfloat16),
        in_specs=[SMEM, VMEM, VMEM],
        out_specs=VMEM,
        compiler_params=params(12),
        cost_estimate=pl.CostEstimate(flops=10**9, bytes_accessed=4 * 10**6, transcendentals=0),
        name="rest_step",
    )(table, x, grad_t)


SWAP = [(0, 1), (1, 0)]


def body(activations, weight_tiles, tile_ids, tile_counts, upstream):
    live = jnp.arange(CAP, dtype=jnp.int32) < tile_counts.reshape(())
    tiles = jnp.where(live[:, None, None], weight_tiles.reshape(CAP, TILE, TILE), 0)
    packed = tiles.reshape(PAIRS, 2, TILE, TILE).transpose(0, 3, 1, 2).reshape(PACK, PAIR)
    ids = tile_ids.reshape(1, CAP)
    block = 2 * lax.axis_index("y") + lax.axis_index("core")
    d = ids // PER_COL
    unit = d // SUB * (NZ * SUB) + block * SUB + d % SUB
    meta = jnp.pad(unit, ((0, META - 1), (0, PAIR - CAP))) + jnp.pad(
        ids % PER_COL, ((0, META - 1), (F_LANE, PAIR - F_LANE - CAP))
    )
    sent = jnp.concatenate([packed, meta.astype(jnp.bfloat16)], axis=0)
    wide = jnp.broadcast_to(sent[None], (NY, ROWS, PAIR))
    w_own = lax.all_to_all(wide, "y", split_axis=0, concat_axis=0, tiled=True)

    x_mine = activations.T.reshape(1, SHARD // 16, 16, TOK)
    x_col = lax.all_gather(x_mine, "z", axis=0, tiled=True).reshape(1, NZ * SHARD, TOK)
    x_wide = jnp.broadcast_to(x_col, (NX, NZ * SHARD, TOK))
    x = lax.all_to_all(x_wide, "x", split_axis=0, concat_axis=0, tiled=True).reshape(X_ROWS, TOK)

    w_other = lax.ppermute(w_own, "core", SWAP)
    table = jnp.concatenate(
        [jnp.sum(w[:, PACK:, :].astype(jnp.float32), axis=1) for w in (w_own, w_other)], axis=0
    ).astype(jnp.int32)
    output, grad, theirs = main_step(table, x, w_own, w_other, upstream)
    arrived = lax.ppermute(theirs, "core", SWAP)
    mine = rest_step(table, x, grad)
    both = (mine.astype(jnp.float32) + arrived.astype(jnp.float32)).astype(jnp.bfloat16)
    parts = lax.all_to_all(both, "y", split_axis=0, concat_axis=0, tiled=True)
    summed = jnp.sum(parts.astype(jnp.float32), axis=0)
    summed = summed.reshape(PAIRS, TILE, 2, TILE).transpose(0, 2, 3, 1).reshape(CAP, TILE * TILE)
    result = jnp.where(live[:, None], summed, 0.0).astype(jnp.bfloat16)
    return output, result.reshape(1, 1, CAP, TILE * TILE)


def solution(mesh):
    fine = Mesh(mesh.devices.reshape(NZ, NX, NY, 2), ("z", "x", "y", "core"))
    rows, cols = ("z", "x"), ("y", "core")
    return jax.shard_map(
        body,
        mesh=fine,
        in_specs=(
            P(cols, rows),
            P(cols, rows, None, None),
            P(cols, rows, None),
            P(cols, rows),
            P(cols, rows),
        ),
        out_specs=(P(cols, rows), P(cols, rows, None, None)),
        check_vma=False,
    )
```

```python
import jax
import jax.numpy as jnp
from jax import lax
from jax.experimental import pallas as pl
from jax.experimental.pallas import tpu as pltpu
from jax.sharding import Mesh, PartitionSpec as P


TILE = 64
PAIR = 2 * TILE
CAP = 12
PAIRS = CAP // 2
PACK = PAIRS * TILE
META = 16
ROWS = PACK + META
PER_COL = 6
SUB = 3
F_LANE = 16
NZ, NX, NY = 16, 4, 8
SHARD = 192
COL_ROWS = NZ * SHARD
CUT = COL_ROWS // 2
X_ROWS = NX * COL_ROWS
FF_LOC = 384
TOK = 128


VMEM = pl.BlockSpec(memory_space=pltpu.VMEM)
ANY = pl.BlockSpec(memory_space=pl.ANY)
SMEM = pl.BlockSpec(memory_space=pltpu.SMEM)


def aligned(start, size):
    return pl.ds(pl.multiple_of(start, size), size)


def lanes_below():
    return lax.broadcasted_iota(jnp.int32, (1, PAIR), 1) < TILE


def two(ref, start0, start1):
    return jnp.concatenate([ref[aligned(start0 * TILE, TILE), :], ref[aligned(start1 * TILE, TILE), :]], axis=0)


def slot_grads(table, b, x, grad_t, dw, y):
    low = lanes_below()
    for m in range(PAIRS):
        s = 2 * m
        cols = two(grad_t, table[b, F_LANE + s], table[b, F_LANE + s + 1])
        rows = two(x, table[b, s], table[b, s + 1])
        prod = lax.dot_general(cols, rows, (((1,), (1,)), ((), ())), preferred_element_type=jnp.float32)
        dw[y, m * TILE : (m + 1) * TILE, :] = jnp.where(low, prod[:TILE], prod[TILE:]).astype(jnp.bfloat16)


def main_kernel(
    table, here, x0, x1a, x1b, x2a, x2b, x3a, x3b, w0, w1, up, out, grad_t, x, dw, acc, tiles0, tiles1, sem
):
    def part(distance, start, size):
        column = (here[0] + distance) & (NX - 1)
        return x.at[pl.ds(pl.multiple_of(column * COL_ROWS + start, CUT), size), :]

    moves = [
        (w0, tiles0),
        (w1, tiles1),
        (x0, part(0, 0, COL_ROWS)),
        (x1a, part(1, 0, CUT)),
        (x1b, part(1, CUT, CUT)),
        (x2a, part(2, 0, CUT)),
        (x2b, part(2, CUT, CUT)),
        (x3a, part(3, 0, CUT)),
        (x3b, part(3, CUT, CUT)),
    ]
    copies = [pltpu.make_async_copy(a, b, sem.at[i]) for i, (a, b) in enumerate(moves)]
    for c in copies:
        c.start()
    acc[...] = jnp.zeros_like(acc)
    for c in copies[2:]:
        c.wait()
    low = lanes_below()
    first = jnp.where(low, 1.0, 0.0).astype(jnp.bfloat16)
    second = jnp.where(low, 0.0, 1.0).astype(jnp.bfloat16)
    for rc, tiles in enumerate((tiles0, tiles1)):
        copies[rc].wait()

        def forward(y, carry, rc=rc, tiles=tiles):
            b = rc * NY + y
            for m in range(PAIRS):
                s = 2 * m
                tile = tiles[y, m * TILE : (m + 1) * TILE, :]
                prod = jnp.dot(
                    jnp.concatenate([tile * first, tile * second], axis=0),
                    two(x, table[b, s], table[b, s + 1]),
                    preferred_element_type=jnp.float32,
                )
                for p in range(2):
                    acc[aligned(table[b, F_LANE + s + p] * TILE, TILE), :] += prod[p * TILE : (p + 1) * TILE]
            return carry

        lax.fori_loop(0, NY, forward, 0)

    pre = acc[...].T
    cumul = 0.5 * (1.0 + lax.erf(pre * 0.7071067811865476))
    density = jnp.exp(-0.5 * pre * pre) * 0.3989422804014327
    out[...] = (pre * cumul).astype(jnp.bfloat16)
    grad_t[...] = (up[...].astype(jnp.float32) * (cumul + pre * density)).T.astype(jnp.bfloat16)

    def backward(y, carry):
        slot_grads(table, NY + y, x, grad_t, dw, y)
        return carry

    lax.fori_loop(0, NY, backward, 0)


def rest_kernel(table, x, grad_t, dw):
    def backward(y, carry):
        slot_grads(table, y, x, grad_t, dw, y)
        return carry

    lax.fori_loop(0, NY, backward, 0)


def params(mib):
    return pltpu.CompilerParams(vmem_limit_bytes=mib << 20)


def main_step(table, here, x0, x1a, x1b, x2a, x2b, x3a, x3b, w0, w1, up):
    return pl.pallas_call(
        main_kernel,
        out_shape=(
            jax.ShapeDtypeStruct((TOK, FF_LOC), jnp.bfloat16),
            jax.ShapeDtypeStruct((FF_LOC, TOK), jnp.bfloat16),
            jax.ShapeDtypeStruct((X_ROWS, TOK), jnp.bfloat16),
            jax.ShapeDtypeStruct((NY, PACK, PAIR), jnp.bfloat16),
        ),
        in_specs=[SMEM, SMEM] + [ANY] * 9 + [VMEM],
        out_specs=(VMEM, VMEM, VMEM, VMEM),
        scratch_shapes=[
            pltpu.VMEM((FF_LOC, TOK), jnp.float32),
            pltpu.VMEM((NY, ROWS, PAIR), jnp.bfloat16),
            pltpu.VMEM((NY, ROWS, PAIR), jnp.bfloat16),
            pltpu.SemaphoreType.DMA((9,)),
        ],
        compiler_params=params(16),
        cost_estimate=pl.CostEstimate(flops=2 * 10**9, bytes_accessed=8 * 10**6, transcendentals=10**5),
        name="main_step",
    )(table, here, x0, x1a, x1b, x2a, x2b, x3a, x3b, w0, w1, up)


def rest_step(table, x, grad_t):
    return pl.pallas_call(
        rest_kernel,
        out_shape=jax.ShapeDtypeStruct((NY, PACK, PAIR), jnp.bfloat16),
        in_specs=[SMEM, VMEM, VMEM],
        out_specs=VMEM,
        compiler_params=params(12),
        cost_estimate=pl.CostEstimate(flops=10**9, bytes_accessed=4 * 10**6, transcendentals=0),
        name="rest_step",
    )(table, x, grad_t)


def ring(n, step):
    return [(i, (i + step) % n) for i in range(n)]


SWAP = [(0, 1), (1, 0)]


def body(activations, weight_tiles, tile_ids, tile_counts, upstream):
    live = jnp.arange(CAP, dtype=jnp.int32) < tile_counts.reshape(())
    tiles = jnp.where(live[:, None, None], weight_tiles.reshape(CAP, TILE, TILE), 0)
    packed = tiles.reshape(PAIRS, 2, TILE, TILE).transpose(0, 3, 1, 2).reshape(PACK, PAIR)
    ids = tile_ids.reshape(1, CAP)
    block = 2 * lax.axis_index("y") + lax.axis_index("core")
    d = ids // PER_COL
    unit = d // SUB * (NZ * SUB) + block * SUB + d % SUB
    meta = jnp.pad(unit, ((0, META - 1), (0, PAIR - CAP))) + jnp.pad(
        ids % PER_COL, ((0, META - 1), (F_LANE, PAIR - F_LANE - CAP))
    )
    sent = jnp.concatenate([packed, meta.astype(jnp.bfloat16)], axis=0)
    wide = jnp.broadcast_to(sent[None], (NY, ROWS, PAIR))
    w_own = lax.all_to_all(wide, "y", split_axis=0, concat_axis=0, tiled=True)

    x_mine = activations.T.reshape(1, SHARD // 16, 16, TOK)
    x0 = lax.all_gather(x_mine, "z", axis=0, tiled=True).reshape(COL_ROWS, TOK)
    lower, upper = x0[:CUT], x0[CUT:]
    up_one, down_one = ring(NX, 1), ring(NX, -1)
    x3a = lax.ppermute(lower, "x", up_one)
    x1b = lax.ppermute(upper, "x", down_one)
    x3b = lax.ppermute(upper, "x", up_one)
    x1a = lax.ppermute(lower, "x", down_one)
    x2a = lax.ppermute(x3a, "x", up_one)
    x2b = lax.ppermute(x1b, "x", down_one)
    w_other = lax.ppermute(w_own, "core", SWAP)

    table = jnp.concatenate(
        [jnp.sum(w[:, PACK:, :].astype(jnp.float32), axis=1) for w in (w_own, w_other)], axis=0
    ).astype(jnp.int32)
    here = lax.axis_index("x").astype(jnp.int32).reshape(1)
    output, grad, x, theirs = main_step(table, here, x0, x1a, x1b, x2a, x2b, x3a, x3b, w_own, w_other, upstream)
    arrived = lax.ppermute(theirs, "core", SWAP)
    mine = rest_step(table, x, grad)
    both = (mine.astype(jnp.float32) + arrived.astype(jnp.float32)).astype(jnp.bfloat16)
    parts = lax.all_to_all(both, "y", split_axis=0, concat_axis=0, tiled=True)
    summed = jnp.sum(parts.astype(jnp.float32), axis=0)
    summed = summed.reshape(PAIRS, TILE, 2, TILE).transpose(0, 2, 3, 1).reshape(CAP, TILE * TILE)
    result = jnp.where(live[:, None], summed, 0.0).astype(jnp.bfloat16)
    return output, result.reshape(1, 1, CAP, TILE * TILE)


def solution(mesh):
    fine = Mesh(mesh.devices.reshape(NZ, NX, NY, 2), ("z", "x", "y", "core"))
    rows, cols = ("z", "x"), ("y", "core")
    return jax.shard_map(
        body,
        mesh=fine,
        in_specs=(
            P(cols, rows),
            P(cols, rows, None, None),
            P(cols, rows, None),
            P(cols, rows),
            P(cols, rows),
        ),
        out_specs=(P(cols, rows), P(cols, rows, None, None)),
        check_vma=False,
    )
```

```python
import jax
import jax.numpy as jnp
from jax import lax
from jax.experimental import pallas as pl
from jax.experimental.pallas import tpu as pltpu
from jax.sharding import Mesh, PartitionSpec as P


TILE = 64
PAIR = 2 * TILE
CAP = 12
PAIRS = CAP // 2
PACK = PAIRS * TILE
META = 16
ROWS = PACK + META
PER_COL = 6
SUB = 3
F_LANE = 16
NZ, NX, NY = 16, 4, 8
SHARD = 192
COL_ROWS = NZ * SHARD
CUT = COL_ROWS // 2
X_ROWS = NX * COL_ROWS
FF_LOC = 384
TOK = 128


VMEM = pl.BlockSpec(memory_space=pltpu.VMEM)
ANY = pl.BlockSpec(memory_space=pl.ANY)
SMEM = pl.BlockSpec(memory_space=pltpu.SMEM)


def aligned(start, size):
    return pl.ds(pl.multiple_of(start, size), size)


def lanes_below():
    return lax.broadcasted_iota(jnp.int32, (1, PAIR), 1) < TILE


def two(ref, start0, start1):
    return jnp.concatenate([ref[aligned(start0 * TILE, TILE), :], ref[aligned(start1 * TILE, TILE), :]], axis=0)


def slot_grads(table, b, x, grad_t, dw, y):
    low = lanes_below()
    for m in range(PAIRS):
        s = 2 * m
        cols = two(grad_t, table[b, F_LANE + s], table[b, F_LANE + s + 1])
        rows = two(x, table[b, s], table[b, s + 1])
        prod = lax.dot_general(cols, rows, (((1,), (1,)), ((), ())), preferred_element_type=jnp.float32)
        dw[y, m * TILE : (m + 1) * TILE, :] = jnp.where(low, prod[:TILE], prod[TILE:]).astype(jnp.bfloat16)


def main_kernel(
    table, here, x0, x1a, x1b, x2a, x2b, x3a, x3b, w0, w1, up, out, grad_t, x, dw, acc, tiles0, tiles1, sem
):
    def part(distance, start, size):
        column = here[0] ^ distance
        return x.at[pl.ds(pl.multiple_of(column * COL_ROWS + start, CUT), size), :]

    moves = [
        (w0, tiles0),
        (w1, tiles1),
        (x0, part(0, 0, COL_ROWS)),
        (x1a, part(1, 0, CUT)),
        (x1b, part(1, CUT, CUT)),
        (x2a, part(2, 0, CUT)),
        (x2b, part(2, CUT, CUT)),
        (x3a, part(3, 0, CUT)),
        (x3b, part(3, CUT, CUT)),
    ]
    copies = [pltpu.make_async_copy(a, b, sem.at[i]) for i, (a, b) in enumerate(moves)]
    for c in copies:
        c.start()
    acc[...] = jnp.zeros_like(acc)
    for c in copies[2:]:
        c.wait()
    low = lanes_below()
    first = jnp.where(low, 1.0, 0.0).astype(jnp.bfloat16)
    second = jnp.where(low, 0.0, 1.0).astype(jnp.bfloat16)
    for rc, tiles in enumerate((tiles0, tiles1)):
        copies[rc].wait()

        def forward(y, carry, rc=rc, tiles=tiles):
            b = rc * NY + y
            for m in range(PAIRS):
                s = 2 * m
                tile = tiles[y, m * TILE : (m + 1) * TILE, :]
                prod = jnp.dot(
                    jnp.concatenate([tile * first, tile * second], axis=0),
                    two(x, table[b, s], table[b, s + 1]),
                    preferred_element_type=jnp.float32,
                )
                for p in range(2):
                    acc[aligned(table[b, F_LANE + s + p] * TILE, TILE), :] += prod[p * TILE : (p + 1) * TILE]
            return carry

        lax.fori_loop(0, NY, forward, 0, unroll=2)

    pre = acc[...].T
    cumul = 0.5 * (1.0 + lax.erf(pre * 0.7071067811865476))
    density = jnp.exp(-0.5 * pre * pre) * 0.3989422804014327
    out[...] = (pre * cumul).astype(jnp.bfloat16)
    grad_t[...] = (up[...].astype(jnp.float32) * (cumul + pre * density)).T.astype(jnp.bfloat16)

    def backward(y, carry):
        slot_grads(table, NY + y, x, grad_t, dw, y)
        return carry

    lax.fori_loop(0, NY, backward, 0, unroll=2)


def rest_kernel(table, x, grad_t, dw):
    def backward(y, carry):
        slot_grads(table, y, x, grad_t, dw, y)
        return carry

    lax.fori_loop(0, NY, backward, 0, unroll=2)


def params(mib):
    return pltpu.CompilerParams(vmem_limit_bytes=mib << 20)


def main_step(table, here, x0, x1a, x1b, x2a, x2b, x3a, x3b, w0, w1, up):
    return pl.pallas_call(
        main_kernel,
        out_shape=(
            jax.ShapeDtypeStruct((TOK, FF_LOC), jnp.bfloat16),
            jax.ShapeDtypeStruct((FF_LOC, TOK), jnp.bfloat16),
            jax.ShapeDtypeStruct((X_ROWS, TOK), jnp.bfloat16),
            jax.ShapeDtypeStruct((NY, PACK, PAIR), jnp.bfloat16),
        ),
        in_specs=[SMEM, SMEM] + [ANY] * 9 + [VMEM],
        out_specs=(VMEM, VMEM, VMEM, VMEM),
        scratch_shapes=[
            pltpu.VMEM((FF_LOC, TOK), jnp.float32),
            pltpu.VMEM((NY, ROWS, PAIR), jnp.bfloat16),
            pltpu.VMEM((NY, ROWS, PAIR), jnp.bfloat16),
            pltpu.SemaphoreType.DMA((9,)),
        ],
        compiler_params=params(16),
        cost_estimate=pl.CostEstimate(flops=2 * 10**9, bytes_accessed=8 * 10**6, transcendentals=10**5),
        name="main_step",
    )(table, here, x0, x1a, x1b, x2a, x2b, x3a, x3b, w0, w1, up)


def rest_step(table, x, grad_t):
    return pl.pallas_call(
        rest_kernel,
        out_shape=jax.ShapeDtypeStruct((NY, PACK, PAIR), jnp.bfloat16),
        in_specs=[SMEM, VMEM, VMEM],
        out_specs=VMEM,
        compiler_params=params(12),
        cost_estimate=pl.CostEstimate(flops=10**9, bytes_accessed=4 * 10**6, transcendentals=0),
        name="rest_step",
    )(table, x, grad_t)


def trade(mask):
    return [(i, i ^ mask) for i in range(NX)]


SWAP = [(0, 1), (1, 0)]


def body(activations, weight_tiles, tile_ids, tile_counts, upstream):
    live = jnp.arange(CAP, dtype=jnp.int32) < tile_counts.reshape(())
    tiles = jnp.where(live[:, None, None], weight_tiles.reshape(CAP, TILE, TILE), 0)
    packed = tiles.reshape(PAIRS, 2, TILE, TILE).transpose(0, 3, 1, 2).reshape(PACK, PAIR)
    ids = tile_ids.reshape(1, CAP)
    block = 2 * lax.axis_index("y") + lax.axis_index("core")
    d = ids // PER_COL
    unit = d // SUB * (NZ * SUB) + block * SUB + d % SUB
    meta = jnp.pad(unit, ((0, META - 1), (0, PAIR - CAP))) + jnp.pad(
        ids % PER_COL, ((0, META - 1), (F_LANE, PAIR - F_LANE - CAP))
    )
    sent = jnp.concatenate([packed, meta.astype(jnp.bfloat16)], axis=0)
    wide = jnp.broadcast_to(sent[None], (NY, ROWS, PAIR))
    w_own = lax.all_to_all(wide, "y", split_axis=0, concat_axis=0, tiled=True)

    x_mine = activations.T.reshape(1, SHARD // 16, 16, TOK)
    x0 = lax.all_gather(x_mine, "z", axis=0, tiled=True).reshape(COL_ROWS, TOK)
    lower, upper = x0[:CUT], x0[CUT:]
    near, far = trade(1), trade(3)
    x1a = lax.ppermute(lower, "x", near)
    x3b = lax.ppermute(upper, "x", far)
    x1b = lax.ppermute(upper, "x", near)
    x3a = lax.ppermute(lower, "x", far)
    x2a = lax.ppermute(x1a, "x", far)
    x2b = lax.ppermute(x3b, "x", near)
    w_other = lax.ppermute(w_own, "core", SWAP)

    table = jnp.concatenate(
        [jnp.sum(w[:, PACK:, :].astype(jnp.float32), axis=1) for w in (w_own, w_other)], axis=0
    ).astype(jnp.int32)
    here = lax.axis_index("x").astype(jnp.int32).reshape(1)
    output, grad, x, theirs = main_step(table, here, x0, x1a, x1b, x2a, x2b, x3a, x3b, w_own, w_other, upstream)
    arrived = lax.ppermute(theirs, "core", SWAP)
    mine = rest_step(table, x, grad)
    both = (mine.astype(jnp.float32) + arrived.astype(jnp.float32)).astype(jnp.bfloat16)
    parts = lax.all_to_all(both, "y", split_axis=0, concat_axis=0, tiled=True)
    summed = jnp.sum(parts.astype(jnp.float32), axis=0)
    summed = summed.reshape(PAIRS, TILE, 2, TILE).transpose(0, 2, 3, 1).reshape(CAP, TILE * TILE)
    result = jnp.where(live[:, None], summed, 0.0).astype(jnp.bfloat16)
    return output, result.reshape(1, 1, CAP, TILE * TILE)


def solution(mesh):
    fine = Mesh(mesh.devices.reshape(NZ, NX, NY, 2), ("z", "x", "y", "core"))
    rows, cols = ("z", "x"), ("y", "core")
    return jax.shard_map(
        body,
        mesh=fine,
        in_specs=(
            P(cols, rows),
            P(cols, rows, None, None),
            P(cols, rows, None),
            P(cols, rows),
            P(cols, rows),
        ),
        out_specs=(P(cols, rows), P(cols, rows, None, None)),
        check_vma=False,
    )
```

```python
import jax
import jax.numpy as jnp
from jax import lax
from jax.experimental import pallas as pl
from jax.experimental.pallas import tpu as pltpu
from jax.sharding import Mesh, PartitionSpec as P


TILE = 64
PAIR = 2 * TILE
CAP = 12
PAIRS = CAP // 2
PACK = PAIRS * TILE
META = 16
ROWS = PACK + META
PER_COL = 6
SUB = 3
F_LANE = 16
NZ, NX, NY = 16, 4, 8
SHARD = 192
COL_ROWS = NZ * SHARD
CUT = COL_ROWS // 2
X_ROWS = NX * COL_ROWS
UNITS = COL_ROWS // TILE
GROUP = 8
FF_LOC = 384
TOK = 128


VMEM = pl.BlockSpec(memory_space=pltpu.VMEM)
ANY = pl.BlockSpec(memory_space=pl.ANY)
SMEM = pl.BlockSpec(memory_space=pltpu.SMEM)


def aligned(start, size):
    return pl.ds(pl.multiple_of(start, size), size)


def lanes_below():
    return lax.broadcasted_iota(jnp.int32, (1, PAIR), 1) < TILE


def two(ref, start0, start1):
    return jnp.concatenate([ref[aligned(start0 * TILE, TILE), :], ref[aligned(start1 * TILE, TILE), :]], axis=0)


def slot_grads(table, b, x, grad_t, dw, y):
    low = lanes_below()
    for m in range(PAIRS):
        s = 2 * m
        cols = two(grad_t, table[b, F_LANE + s], table[b, F_LANE + s + 1])
        rows = two(x, table[b, s], table[b, s + 1])
        prod = lax.dot_general(cols, rows, (((1,), (1,)), ((), ())), preferred_element_type=jnp.float32)
        dw[y, m * TILE : (m + 1) * TILE, :] = jnp.where(low, prod[:TILE], prod[TILE:]).astype(jnp.bfloat16)


def lane_masks():
    low = lanes_below()
    return jnp.where(low, 1.0, 0.0).astype(jnp.bfloat16), jnp.where(low, 0.0, 1.0).astype(jnp.bfloat16)


def early_kernel(table, here, x0, x1a, x1b, x3a, x3b, w0, w1, x, tiles, acc, todo, sem):
    opposite = here[0] ^ 2
    x[pl.ds(pl.multiple_of(opposite * COL_ROWS, COL_ROWS), COL_ROWS), :] = jnp.zeros((COL_ROWS, TOK), jnp.bfloat16)

    def part(distance, start, size):
        column = here[0] ^ distance
        return x.at[pl.ds(pl.multiple_of(column * COL_ROWS + start, CUT), size), :]

    moves = [
        (x0, part(0, 0, COL_ROWS)),
        (x1a, part(1, 0, CUT)),
        (x1b, part(1, CUT, CUT)),
        (x3a, part(3, 0, CUT)),
        (x3b, part(3, CUT, CUT)),
        (w0, tiles.at[0:NY]),
        (w1, tiles.at[NY : 2 * NY]),
    ]
    copies = [pltpu.make_async_copy(a, b, sem.at[i]) for i, (a, b) in enumerate(moves)]
    for c in copies:
        c.start()
    acc[...] = jnp.zeros_like(acc)

    def sort_out(b, n):
        for s in range(CAP):
            todo[0, n] = b * 16 + s
            todo[1, n] = table[b, F_LANE + s]
            ahead = table[b, s] - opposite * UNITS
            n = n + jnp.where((ahead >= 0) & (ahead < UNITS), 1, 0)
        return n

    count = lax.fori_loop(0, 2 * NY, sort_out, 0)
    for i in range(GROUP):
        todo[0, count + i] = 0
        todo[1, count + i] = PER_COL
    todo[2, 0] = count
    first, second = lane_masks()
    for c in copies:
        c.wait()

    def forward(b, carry):
        for m in range(PAIRS):
            s = 2 * m
            tile = tiles[b, m * TILE : (m + 1) * TILE, :]
            prod = jnp.dot(
                jnp.concatenate([tile * first, tile * second], axis=0),
                two(x, table[b, s], table[b, s + 1]),
                preferred_element_type=jnp.float32,
            )
            for p in range(2):
                acc[aligned(table[b, F_LANE + s + p] * TILE, TILE), :] += prod[p * TILE : (p + 1) * TILE]
        return carry

    lax.fori_loop(0, 2 * NY, forward, 0, unroll=2)


def main_kernel(table, here, todo, x_in, tiles, acc_in, x2a, x2b, up, out, grad_t, x, dw, acc, sem):
    base = (here[0] ^ 2) * COL_ROWS
    copies = [
        pltpu.make_async_copy(x2a, x.at[pl.ds(pl.multiple_of(base, CUT), CUT), :], sem.at[0]),
        pltpu.make_async_copy(x2b, x.at[pl.ds(pl.multiple_of(base + CUT, CUT), CUT), :], sem.at[1]),
    ]
    for c in copies:
        c.start()
    acc[...] = acc_in[...]
    first, second = lane_masks()
    for c in copies:
        c.wait()

    def forward(g, carry):
        for i in range(GROUP):
            j = todo[0, g * GROUP + i]
            b, s = j >> 4, j & 15
            m = s >> 1
            tile = tiles[b, aligned(m * TILE, TILE), :]
            prod = jnp.dot(
                tile * jnp.where((s & 1) == 0, first, second),
                two(x, table[b, 2 * m], table[b, 2 * m + 1]),
                preferred_element_type=jnp.float32,
            )
            acc[aligned(todo[1, g * GROUP + i] * TILE, TILE), :] += prod
        return carry

    lax.fori_loop(0, (todo[2, 0] + GROUP - 1) // GROUP, forward, 0)
    pre = acc[:FF_LOC].T
    cumul = 0.5 * (1.0 + lax.erf(pre * 0.7071067811865476))
    density = jnp.exp(-0.5 * pre * pre) * 0.3989422804014327
    out[...] = (pre * cumul).astype(jnp.bfloat16)
    grad_t[...] = (up[...].astype(jnp.float32) * (cumul + pre * density)).T.astype(jnp.bfloat16)

    def backward(y, carry):
        slot_grads(table, NY + y, x, grad_t, dw, y)
        return carry

    lax.fori_loop(0, NY, backward, 0, unroll=2)


def rest_kernel(table, x, grad_t, dw):
    def backward(y, carry):
        slot_grads(table, y, x, grad_t, dw, y)
        return carry

    lax.fori_loop(0, NY, backward, 0, unroll=2)


def params(mib):
    return pltpu.CompilerParams(vmem_limit_bytes=mib << 20)


def early_step(table, here, *parts):
    return pl.pallas_call(
        early_kernel,
        out_shape=(
            jax.ShapeDtypeStruct((X_ROWS, TOK), jnp.bfloat16),
            jax.ShapeDtypeStruct((2 * NY, ROWS, PAIR), jnp.bfloat16),
            jax.ShapeDtypeStruct((FF_LOC + TILE, TOK), jnp.float32),
            jax.ShapeDtypeStruct((3, 256), jnp.int32),
        ),
        in_specs=[SMEM, SMEM] + [ANY] * 7,
        out_specs=(VMEM, VMEM, VMEM, SMEM),
        scratch_shapes=[pltpu.SemaphoreType.DMA((7,))],
        compiler_params=params(12),
        cost_estimate=pl.CostEstimate(flops=10**9, bytes_accessed=8 * 10**6, transcendentals=0),
        name="early_step",
    )(table, here, *parts)


def main_step(table, here, todo, x, tiles, acc, x2a, x2b, up):
    return pl.pallas_call(
        main_kernel,
        out_shape=(
            jax.ShapeDtypeStruct((TOK, FF_LOC), jnp.bfloat16),
            jax.ShapeDtypeStruct((FF_LOC, TOK), jnp.bfloat16),
            jax.ShapeDtypeStruct((X_ROWS, TOK), jnp.bfloat16),
            jax.ShapeDtypeStruct((NY, PACK, PAIR), jnp.bfloat16),
        ),
        in_specs=[SMEM, SMEM, SMEM, VMEM, VMEM, VMEM, ANY, ANY, VMEM],
        out_specs=(VMEM, VMEM, VMEM, VMEM),
        scratch_shapes=[pltpu.VMEM((FF_LOC + TILE, TOK), jnp.float32), pltpu.SemaphoreType.DMA((2,))],
        input_output_aliases={3: 2},
        compiler_params=params(14),
        cost_estimate=pl.CostEstimate(flops=10**9, bytes_accessed=8 * 10**6, transcendentals=10**5),
        name="main_step",
    )(table, here, todo, x, tiles, acc, x2a, x2b, up)


def rest_step(table, x, grad_t):
    return pl.pallas_call(
        rest_kernel,
        out_shape=jax.ShapeDtypeStruct((NY, PACK, PAIR), jnp.bfloat16),
        in_specs=[SMEM, VMEM, VMEM],
        out_specs=VMEM,
        compiler_params=params(12),
        cost_estimate=pl.CostEstimate(flops=10**9, bytes_accessed=4 * 10**6, transcendentals=0),
        name="rest_step",
    )(table, x, grad_t)


def trade(mask):
    return [(i, i ^ mask) for i in range(NX)]


SWAP = [(0, 1), (1, 0)]


def body(activations, weight_tiles, tile_ids, tile_counts, upstream):
    live = jnp.arange(CAP, dtype=jnp.int32) < tile_counts.reshape(())
    tiles = jnp.where(live[:, None, None], weight_tiles.reshape(CAP, TILE, TILE), 0)
    packed = tiles.reshape(PAIRS, 2, TILE, TILE).transpose(0, 3, 1, 2).reshape(PACK, PAIR)
    ids = tile_ids.reshape(1, CAP)
    block = 2 * lax.axis_index("y") + lax.axis_index("core")
    d = ids // PER_COL
    unit = d // SUB * (NZ * SUB) + block * SUB + d % SUB
    meta = jnp.pad(unit, ((0, META - 1), (0, PAIR - CAP))) + jnp.pad(
        ids % PER_COL, ((0, META - 1), (F_LANE, PAIR - F_LANE - CAP))
    )
    sent = jnp.concatenate([packed, meta.astype(jnp.bfloat16)], axis=0)
    wide = jnp.broadcast_to(sent[None], (NY, ROWS, PAIR))
    w_own = lax.all_to_all(wide, "y", split_axis=0, concat_axis=0, tiled=True)

    x_mine = activations.T.reshape(1, SHARD // 16, 16, TOK)
    x0 = lax.all_gather(x_mine, "z", axis=0, tiled=True).reshape(COL_ROWS, TOK)
    lower, upper = x0[:CUT], x0[CUT:]
    near, far = trade(1), trade(3)
    x1a = lax.ppermute(lower, "x", near)
    x3b = lax.ppermute(upper, "x", far)
    x1b = lax.ppermute(upper, "x", near)
    x3a = lax.ppermute(lower, "x", far)
    x2a = lax.ppermute(x1a, "x", far)
    x2b = lax.ppermute(x3b, "x", near)
    w_other = lax.ppermute(w_own, "core", SWAP)

    table = jnp.concatenate(
        [jnp.sum(w[:, PACK:, :].astype(jnp.float32), axis=1) for w in (w_own, w_other)], axis=0
    ).astype(jnp.int32)
    here = lax.axis_index("x").astype(jnp.int32).reshape(1)
    x, tiles, acc, todo = early_step(table, here, x0, x1a, x1b, x3a, x3b, w_own, w_other)
    output, grad, x, theirs = main_step(table, here, todo, x, tiles, acc, x2a, x2b, upstream)
    arrived = lax.ppermute(theirs, "core", SWAP)
    mine = rest_step(table, x, grad)
    both = (mine.astype(jnp.float32) + arrived.astype(jnp.float32)).astype(jnp.bfloat16)
    parts = lax.all_to_all(both, "y", split_axis=0, concat_axis=0, tiled=True)
    summed = jnp.sum(parts.astype(jnp.float32), axis=0)
    summed = summed.reshape(PAIRS, TILE, 2, TILE).transpose(0, 2, 3, 1).reshape(CAP, TILE * TILE)
    result = jnp.where(live[:, None], summed, 0.0).astype(jnp.bfloat16)
    return output, result.reshape(1, 1, CAP, TILE * TILE)


def solution(mesh):
    fine = Mesh(mesh.devices.reshape(NZ, NX, NY, 2), ("z", "x", "y", "core"))
    rows, cols = ("z", "x"), ("y", "core")
    return jax.shard_map(
        body,
        mesh=fine,
        in_specs=(
            P(cols, rows),
            P(cols, rows, None, None),
            P(cols, rows, None),
            P(cols, rows),
            P(cols, rows),
        ),
        out_specs=(P(cols, rows), P(cols, rows, None, None)),
        check_vma=False,
    )
```

```python
import jax
import jax.numpy as jnp
from jax import lax
from jax.experimental import pallas as pl
from jax.experimental.pallas import tpu as pltpu
from jax.sharding import Mesh, PartitionSpec as P


TILE = 64
PAIR = 2 * TILE
CAP = 12
PAIRS = CAP // 2
PACK = PAIRS * TILE
META = 16
ROWS = PACK + META
PER_COL = 6
SUB = 3
F_LANE = 16
NZ, NX, NY = 16, 4, 8
SHARD = 192
COL_ROWS = NZ * SHARD
CUT = COL_ROWS // 2
X_ROWS = NX * COL_ROWS
UNITS = COL_ROWS // TILE
GROUP = 8
FF_LOC = 384
TOK = 128


VMEM = pl.BlockSpec(memory_space=pltpu.VMEM)
ANY = pl.BlockSpec(memory_space=pl.ANY)
SMEM = pl.BlockSpec(memory_space=pltpu.SMEM)


def aligned(start, size):
    return pl.ds(pl.multiple_of(start, size), size)


def lanes_below():
    return lax.broadcasted_iota(jnp.int32, (1, PAIR), 1) < TILE


def two(ref, start0, start1):
    return jnp.concatenate([ref[aligned(start0 * TILE, TILE), :], ref[aligned(start1 * TILE, TILE), :]], axis=0)


def slot_grads(table, b, x, grad_t, dw, y):
    low = lanes_below()
    for m in range(PAIRS):
        s = 2 * m
        cols = two(grad_t, table[b, F_LANE + s], table[b, F_LANE + s + 1])
        rows = two(x, table[b, s], table[b, s + 1])
        prod = lax.dot_general(cols, rows, (((1,), (1,)), ((), ())), preferred_element_type=jnp.float32)
        dw[y, m * TILE : (m + 1) * TILE, :] = jnp.where(low, prod[:TILE], prod[TILE:]).astype(jnp.bfloat16)


def lane_masks():
    low = lanes_below()
    return jnp.where(low, 1.0, 0.0).astype(jnp.bfloat16), jnp.where(low, 0.0, 1.0).astype(jnp.bfloat16)


def pack_kernel(ids, count, tiles, wide, sent, sem):
    for m in range(PAIRS):
        halves = [
            jnp.where(2 * m + p < count[0, 0], tiles[2 * m + p].astype(jnp.float32).T, 0.0) for p in range(2)
        ]
        sent[m * TILE : (m + 1) * TILE, :] = jnp.concatenate(halves, axis=1).astype(jnp.bfloat16)
    block = 2 * lax.axis_index("y") + lax.axis_index("core")
    row = lax.broadcasted_iota(jnp.int32, (META, PAIR), 0)
    lane = lax.broadcasted_iota(jnp.int32, (META, PAIR), 1)
    meta = jnp.zeros((META, PAIR), jnp.int32)
    for s in range(CAP):
        d = (ids[0, s] * 43) >> 8
        column = (d * 86) >> 8
        meta = jnp.where(lane == s, column * UNITS + block * SUB + d - column * SUB, meta)
        meta = jnp.where(lane == F_LANE + s, ids[0, s] - d * PER_COL, meta)
    sent[PACK:, :] = jnp.where(row == 0, meta, 0).astype(jnp.float32).astype(jnp.bfloat16)
    copies = [pltpu.make_async_copy(sent, wide.at[y], sem.at[y]) for y in range(NY)]
    for c in copies:
        c.start()
    for c in copies:
        c.wait()


def early_kernel(table, here, x0, x1a, x1b, x3a, x3b, w0, w1, x, tiles, acc, todo, sem):
    opposite = here[0] ^ 2
    x[pl.ds(pl.multiple_of(opposite * COL_ROWS, COL_ROWS), COL_ROWS), :] = jnp.zeros((COL_ROWS, TOK), jnp.bfloat16)

    def part(distance, start, size):
        column = here[0] ^ distance
        return x.at[pl.ds(pl.multiple_of(column * COL_ROWS + start, CUT), size), :]

    moves = [
        (x0, part(0, 0, COL_ROWS)),
        (x1a, part(1, 0, CUT)),
        (x1b, part(1, CUT, CUT)),
        (x3a, part(3, 0, CUT)),
        (x3b, part(3, CUT, CUT)),
        (w0, tiles.at[0:NY]),
        (w1, tiles.at[NY : 2 * NY]),
    ]
    copies = [pltpu.make_async_copy(a, b, sem.at[i]) for i, (a, b) in enumerate(moves)]
    for c in copies:
        c.start()
    acc[...] = jnp.zeros_like(acc)

    def sort_out(b, n):
        for s in range(CAP):
            todo[0, n] = b * 16 + s
            todo[1, n] = table[b, F_LANE + s]
            ahead = table[b, s] - opposite * UNITS
            n = n + jnp.where((ahead >= 0) & (ahead < UNITS), 1, 0)
        return n

    count = lax.fori_loop(0, 2 * NY, sort_out, 0)
    for i in range(GROUP):
        todo[0, count + i] = 0
        todo[1, count + i] = PER_COL
    todo[2, 0] = count
    first, second = lane_masks()
    for c in copies:
        c.wait()

    def forward(b, carry):
        for m in range(PAIRS):
            s = 2 * m
            tile = tiles[b, m * TILE : (m + 1) * TILE, :]
            prod = jnp.dot(
                jnp.concatenate([tile * first, tile * second], axis=0),
                two(x, table[b, s], table[b, s + 1]),
                preferred_element_type=jnp.float32,
            )
            for p in range(2):
                acc[aligned(table[b, F_LANE + s + p] * TILE, TILE), :] += prod[p * TILE : (p + 1) * TILE]
        return carry

    lax.fori_loop(0, 2 * NY, forward, 0, unroll=4)


def main_kernel(table, here, todo, x_in, tiles, acc_in, x2a, x2b, up, out, grad_t, x, dw, acc, sem):
    base = (here[0] ^ 2) * COL_ROWS
    copies = [
        pltpu.make_async_copy(x2a, x.at[pl.ds(pl.multiple_of(base, CUT), CUT), :], sem.at[0]),
        pltpu.make_async_copy(x2b, x.at[pl.ds(pl.multiple_of(base + CUT, CUT), CUT), :], sem.at[1]),
    ]
    for c in copies:
        c.start()
    acc[...] = acc_in[...]
    first, second = lane_masks()
    for c in copies:
        c.wait()

    def forward(g, carry):
        for i in range(GROUP):
            j = todo[0, g * GROUP + i]
            b, s = j >> 4, j & 15
            m = s >> 1
            tile = tiles[b, aligned(m * TILE, TILE), :]
            prod = jnp.dot(
                tile * jnp.where((s & 1) == 0, first, second),
                two(x, table[b, 2 * m], table[b, 2 * m + 1]),
                preferred_element_type=jnp.float32,
            )
            acc[aligned(todo[1, g * GROUP + i] * TILE, TILE), :] += prod
        return carry

    lax.fori_loop(0, (todo[2, 0] + GROUP - 1) // GROUP, forward, 0)
    pre = acc[:FF_LOC].T
    cumul = 0.5 * (1.0 + lax.erf(pre * 0.7071067811865476))
    density = jnp.exp(-0.5 * pre * pre) * 0.3989422804014327
    out[...] = (pre * cumul).astype(jnp.bfloat16)
    grad_t[...] = (up[...].astype(jnp.float32) * (cumul + pre * density)).T.astype(jnp.bfloat16)

    def backward(y, carry):
        slot_grads(table, NY + y, x, grad_t, dw, y)
        return carry

    lax.fori_loop(0, NY, backward, 0, unroll=4)


def rest_kernel(table, x, grad_t, dw):
    def backward(y, carry):
        slot_grads(table, y, x, grad_t, dw, y)
        return carry

    lax.fori_loop(0, NY, backward, 0, unroll=4)


def params(mib):
    return pltpu.CompilerParams(vmem_limit_bytes=mib << 20)


def pack_step(ids, count, tiles):
    return pl.pallas_call(
        pack_kernel,
        out_shape=jax.ShapeDtypeStruct((NY, ROWS, PAIR), jnp.bfloat16),
        in_specs=[SMEM, SMEM, VMEM],
        out_specs=ANY,
        scratch_shapes=[pltpu.VMEM((ROWS, PAIR), jnp.bfloat16), pltpu.SemaphoreType.DMA((NY,))],
        compiler_params=params(4),
        cost_estimate=pl.CostEstimate(flops=10**5, bytes_accessed=10**6, transcendentals=0),
        name="pack_step",
    )(ids, count, tiles)


def early_step(table, here, *parts):
    return pl.pallas_call(
        early_kernel,
        out_shape=(
            jax.ShapeDtypeStruct((X_ROWS, TOK), jnp.bfloat16),
            jax.ShapeDtypeStruct((2 * NY, ROWS, PAIR), jnp.bfloat16),
            jax.ShapeDtypeStruct((FF_LOC + TILE, TOK), jnp.float32),
            jax.ShapeDtypeStruct((3, 256), jnp.int32),
        ),
        in_specs=[SMEM, SMEM] + [ANY] * 7,
        out_specs=(VMEM, VMEM, VMEM, SMEM),
        scratch_shapes=[pltpu.SemaphoreType.DMA((7,))],
        compiler_params=params(12),
        cost_estimate=pl.CostEstimate(flops=10**9, bytes_accessed=8 * 10**6, transcendentals=0),
        name="early_step",
    )(table, here, *parts)


def main_step(table, here, todo, x, tiles, acc, x2a, x2b, up):
    return pl.pallas_call(
        main_kernel,
        out_shape=(
            jax.ShapeDtypeStruct((TOK, FF_LOC), jnp.bfloat16),
            jax.ShapeDtypeStruct((FF_LOC, TOK), jnp.bfloat16),
            jax.ShapeDtypeStruct((X_ROWS, TOK), jnp.bfloat16),
            jax.ShapeDtypeStruct((NY, PACK, PAIR), jnp.bfloat16),
        ),
        in_specs=[SMEM, SMEM, SMEM, VMEM, VMEM, VMEM, ANY, ANY, VMEM],
        out_specs=(VMEM, VMEM, VMEM, VMEM),
        scratch_shapes=[pltpu.VMEM((FF_LOC + TILE, TOK), jnp.float32), pltpu.SemaphoreType.DMA((2,))],
        input_output_aliases={3: 2},
        compiler_params=params(14),
        cost_estimate=pl.CostEstimate(flops=10**9, bytes_accessed=8 * 10**6, transcendentals=10**5),
        name="main_step",
    )(table, here, todo, x, tiles, acc, x2a, x2b, up)


def rest_step(table, x, grad_t):
    return pl.pallas_call(
        rest_kernel,
        out_shape=jax.ShapeDtypeStruct((NY, PACK, PAIR), jnp.bfloat16),
        in_specs=[SMEM, VMEM, VMEM],
        out_specs=VMEM,
        compiler_params=params(12),
        cost_estimate=pl.CostEstimate(flops=10**9, bytes_accessed=4 * 10**6, transcendentals=0),
        name="rest_step",
    )(table, x, grad_t)


def trade(mask):
    return [(i, i ^ mask) for i in range(NX)]


SWAP = [(0, 1), (1, 0)]


def body(activations, weight_tiles, tile_ids, tile_counts, upstream):
    live = jnp.arange(CAP, dtype=jnp.int32) < tile_counts.reshape(())
    wide = pack_step(tile_ids.reshape(1, CAP), tile_counts, weight_tiles.reshape(CAP, TILE, TILE))
    w_own = lax.all_to_all(wide, "y", split_axis=0, concat_axis=0, tiled=True)

    x_mine = activations.T.reshape(1, SHARD // 16, 16, TOK)
    x0 = lax.all_gather(x_mine, "z", axis=0, tiled=True).reshape(COL_ROWS, TOK)
    lower, upper = x0[:CUT], x0[CUT:]
    near, far = trade(1), trade(3)
    x1a = lax.ppermute(lower, "x", near)
    x3b = lax.ppermute(upper, "x", far)
    x1b = lax.ppermute(upper, "x", near)
    x3a = lax.ppermute(lower, "x", far)
    x2a = lax.ppermute(x1a, "x", far)
    x2b = lax.ppermute(x3b, "x", near)
    w_other = lax.ppermute(w_own, "core", SWAP)

    table = jnp.concatenate(
        [jnp.sum(w[:, PACK:, :].astype(jnp.float32), axis=1) for w in (w_own, w_other)], axis=0
    ).astype(jnp.int32)
    here = lax.axis_index("x").astype(jnp.int32).reshape(1)
    x, tiles, acc, todo = early_step(table, here, x0, x1a, x1b, x3a, x3b, w_own, w_other)
    output, grad, x, theirs = main_step(table, here, todo, x, tiles, acc, x2a, x2b, upstream)
    arrived = lax.ppermute(theirs, "core", SWAP)
    mine = rest_step(table, x, grad)
    both = (mine.astype(jnp.float32) + arrived.astype(jnp.float32)).astype(jnp.bfloat16)
    parts = lax.all_to_all(both, "y", split_axis=0, concat_axis=0, tiled=True)
    summed = jnp.sum(parts.astype(jnp.float32), axis=0)
    summed = summed.reshape(PAIRS, TILE, 2, TILE).transpose(0, 2, 3, 1).reshape(CAP, TILE * TILE)
    result = jnp.where(live[:, None], summed, 0.0).astype(jnp.bfloat16)
    return output, result.reshape(1, 1, CAP, TILE * TILE)


def solution(mesh):
    fine = Mesh(mesh.devices.reshape(NZ, NX, NY, 2), ("z", "x", "y", "core"))
    rows, cols = ("z", "x"), ("y", "core")
    return jax.shard_map(
        body,
        mesh=fine,
        in_specs=(
            P(cols, rows),
            P(cols, rows, None, None),
            P(cols, rows, None),
            P(cols, rows),
            P(cols, rows),
        ),
        out_specs=(P(cols, rows), P(cols, rows, None, None)),
        check_vma=False,
    )
```

```python
import jax
import jax.numpy as jnp
from jax import lax
from jax.experimental import pallas as pl
from jax.experimental.pallas import tpu as pltpu
from jax.sharding import Mesh, PartitionSpec as P


TILE = 64
PAIR = 2 * TILE
CAP = 12
PAIRS = CAP // 2
PACK = PAIRS * TILE
META = 16
ROWS = PACK + META
PER_COL = 6
SUB = 3
F_LANE = 16
NZ, NX, NY = 16, 4, 8
SHARD = 192
COL_ROWS = NZ * SHARD
CUT = COL_ROWS // 2
X_ROWS = NX * COL_ROWS
UNITS = COL_ROWS // TILE
GROUP = 8
FF_LOC = 384
TOK = 128


VMEM = pl.BlockSpec(memory_space=pltpu.VMEM)
ANY = pl.BlockSpec(memory_space=pl.ANY)
SMEM = pl.BlockSpec(memory_space=pltpu.SMEM)


def aligned(start, size):
    return pl.ds(pl.multiple_of(start, size), size)


def lanes_below():
    return lax.broadcasted_iota(jnp.int32, (1, PAIR), 1) < TILE


def two(ref, start0, start1):
    return jnp.concatenate([ref[aligned(start0 * TILE, TILE), :], ref[aligned(start1 * TILE, TILE), :]], axis=0)


def slot_grads(table, x, grad_t, dw, b):
    low = lanes_below()
    for m in range(PAIRS):
        s = 2 * m
        cols = two(grad_t, table[b, F_LANE + s], table[b, F_LANE + s + 1])
        rows = two(x, table[b, s], table[b, s + 1])
        prod = lax.dot_general(cols, rows, (((1,), (1,)), ((), ())), preferred_element_type=jnp.float32)
        dw[b, m * TILE : (m + 1) * TILE, :] = jnp.where(low, prod[:TILE], prod[TILE:]).astype(jnp.bfloat16)


def lane_masks():
    low = lanes_below()
    return jnp.where(low, 1.0, 0.0).astype(jnp.bfloat16), jnp.where(low, 0.0, 1.0).astype(jnp.bfloat16)


def list_slots(table, opposite, todo):
    def sort_out(b, n):
        for s in range(CAP):
            todo[0, n] = b * 16 + s
            todo[1, n] = table[b, F_LANE + s]
            ahead = table[b, s] - opposite * UNITS
            n = n + jnp.where((ahead >= 0) & (ahead < UNITS), 1, 0)
        return n

    count = lax.fori_loop(0, NY, sort_out, 0)
    for i in range(GROUP):
        todo[0, count + i] = 0
        todo[1, count + i] = PER_COL
    todo[2, 0] = count


def add_blocks(table, tiles, x, acc):
    first, second = lane_masks()

    def forward(b, carry):
        for m in range(PAIRS):
            s = 2 * m
            tile = tiles[b, m * TILE : (m + 1) * TILE, :]
            prod = jnp.dot(
                jnp.concatenate([tile * first, tile * second], axis=0),
                two(x, table[b, s], table[b, s + 1]),
                preferred_element_type=jnp.float32,
            )
            for p in range(2):
                acc[aligned(table[b, F_LANE + s + p] * TILE, TILE), :] += prod[p * TILE : (p + 1) * TILE]
        return carry

    lax.fori_loop(0, NY, forward, 0, unroll=4)


def add_listed(todo, table, tiles, x, acc):
    first, second = lane_masks()

    def forward(g, carry):
        for i in range(GROUP):
            j = todo[0, g * GROUP + i]
            b, s = j >> 4, j & 15
            m = s >> 1
            tile = tiles[b, aligned(m * TILE, TILE), :]
            prod = jnp.dot(
                tile * jnp.where((s & 1) == 0, first, second),
                two(x, table[b, 2 * m], table[b, 2 * m + 1]),
                preferred_element_type=jnp.float32,
            )
            acc[aligned(todo[1, g * GROUP + i] * TILE, TILE), :] += prod
        return carry

    lax.fori_loop(0, (todo[2, 0] + GROUP - 1) // GROUP, forward, 0)


def own_kernel(table, here, x0, x1a, x1b, x3a, x3b, w, x, tiles, acc, todo, sem):
    opposite = here[0] ^ 2
    x[pl.ds(pl.multiple_of(opposite * COL_ROWS, COL_ROWS), COL_ROWS), :] = jnp.zeros((COL_ROWS, TOK), jnp.bfloat16)

    def part(distance, start, size):
        column = here[0] ^ distance
        return x.at[pl.ds(pl.multiple_of(column * COL_ROWS + start, CUT), size), :]

    moves = [
        (x0, part(0, 0, COL_ROWS)),
        (x1a, part(1, 0, CUT)),
        (x1b, part(1, CUT, CUT)),
        (x3a, part(3, 0, CUT)),
        (x3b, part(3, CUT, CUT)),
        (w, tiles),
    ]
    copies = [pltpu.make_async_copy(a, b, sem.at[i]) for i, (a, b) in enumerate(moves)]
    for c in copies:
        c.start()
    acc[...] = jnp.zeros_like(acc)
    list_slots(table, opposite, todo)
    for c in copies:
        c.wait()
    add_blocks(table, tiles, x, acc)


def other_kernel(table, here, x, acc_in, w, tiles, acc, todo, sem):
    copy = pltpu.make_async_copy(w, tiles, sem.at[0])
    copy.start()
    acc[...] = acc_in[...]
    list_slots(table, here[0] ^ 2, todo)
    copy.wait()
    add_blocks(table, tiles, x, acc)


def main_kernel(
    table0, table1, here, todo0, todo1, x_in, tiles0, tiles1, acc_in, x2a, x2b, up, out, grad_t, x, dw, acc, sem
):
    base = (here[0] ^ 2) * COL_ROWS
    copies = [
        pltpu.make_async_copy(x2a, x.at[pl.ds(pl.multiple_of(base, CUT), CUT), :], sem.at[0]),
        pltpu.make_async_copy(x2b, x.at[pl.ds(pl.multiple_of(base + CUT, CUT), CUT), :], sem.at[1]),
    ]
    for c in copies:
        c.start()
    acc[...] = acc_in[...]
    for c in copies:
        c.wait()
    add_listed(todo0, table0, tiles0, x, acc)
    add_listed(todo1, table1, tiles1, x, acc)
    pre = acc[:FF_LOC].T
    cumul = 0.5 * (1.0 + lax.erf(pre * 0.7071067811865476))
    density = jnp.exp(-0.5 * pre * pre) * 0.3989422804014327
    out[...] = (pre * cumul).astype(jnp.bfloat16)
    grad_t[...] = (up[...].astype(jnp.float32) * (cumul + pre * density)).T.astype(jnp.bfloat16)

    def backward(y, carry):
        slot_grads(table1, x, grad_t, dw, y)
        return carry

    lax.fori_loop(0, NY, backward, 0, unroll=4)


def rest_kernel(table, x, grad_t, dw):
    def backward(y, carry):
        slot_grads(table, x, grad_t, dw, y)
        return carry

    lax.fori_loop(0, NY, backward, 0, unroll=4)


def params(mib):
    return pltpu.CompilerParams(vmem_limit_bytes=mib << 20)


X_SHAPE = jax.ShapeDtypeStruct((X_ROWS, TOK), jnp.bfloat16)
TILES_SHAPE = jax.ShapeDtypeStruct((NY, ROWS, PAIR), jnp.bfloat16)
ACC_SHAPE = jax.ShapeDtypeStruct((FF_LOC + TILE, TOK), jnp.float32)
TODO_SHAPE = jax.ShapeDtypeStruct((3, 128), jnp.int32)


def own_step(table, here, *parts):
    return pl.pallas_call(
        own_kernel,
        out_shape=(X_SHAPE, TILES_SHAPE, ACC_SHAPE, TODO_SHAPE),
        in_specs=[SMEM, SMEM] + [ANY] * 6,
        out_specs=(VMEM, VMEM, VMEM, SMEM),
        scratch_shapes=[pltpu.SemaphoreType.DMA((6,))],
        compiler_params=params(12),
        cost_estimate=pl.CostEstimate(flops=5 * 10**8, bytes_accessed=6 * 10**6, transcendentals=0),
        name="own_step",
    )(table, here, *parts)


def other_step(table, here, x, acc, w):
    return pl.pallas_call(
        other_kernel,
        out_shape=(TILES_SHAPE, ACC_SHAPE, TODO_SHAPE),
        in_specs=[SMEM, SMEM, VMEM, VMEM, ANY],
        out_specs=(VMEM, VMEM, SMEM),
        scratch_shapes=[pltpu.SemaphoreType.DMA((1,))],
        compiler_params=params(12),
        cost_estimate=pl.CostEstimate(flops=5 * 10**8, bytes_accessed=4 * 10**6, transcendentals=0),
        name="other_step",
    )(table, here, x, acc, w)


def main_step(*operands):
    return pl.pallas_call(
        main_kernel,
        out_shape=(
            jax.ShapeDtypeStruct((TOK, FF_LOC), jnp.bfloat16),
            jax.ShapeDtypeStruct((FF_LOC, TOK), jnp.bfloat16),
            X_SHAPE,
            jax.ShapeDtypeStruct((NY, PACK, PAIR), jnp.bfloat16),
        ),
        in_specs=[SMEM] * 5 + [VMEM] * 4 + [ANY, ANY, VMEM],
        out_specs=(VMEM, VMEM, VMEM, VMEM),
        scratch_shapes=[pltpu.VMEM((FF_LOC + TILE, TOK), jnp.float32), pltpu.SemaphoreType.DMA((2,))],
        input_output_aliases={5: 2},
        compiler_params=params(14),
        cost_estimate=pl.CostEstimate(flops=10**9, bytes_accessed=8 * 10**6, transcendentals=10**5),
        name="main_step",
    )(*operands)


def rest_step(table, x, grad_t):
    return pl.pallas_call(
        rest_kernel,
        out_shape=jax.ShapeDtypeStruct((NY, PACK, PAIR), jnp.bfloat16),
        in_specs=[SMEM, VMEM, VMEM],
        out_specs=VMEM,
        compiler_params=params(12),
        cost_estimate=pl.CostEstimate(flops=10**9, bytes_accessed=4 * 10**6, transcendentals=0),
        name="rest_step",
    )(table, x, grad_t)


def trade(mask):
    return [(i, i ^ mask) for i in range(NX)]


SWAP = [(0, 1), (1, 0)]


def body(activations, weight_tiles, tile_ids, tile_counts, upstream):
    live = jnp.arange(CAP, dtype=jnp.int32) < tile_counts.reshape(())
    tiles = jnp.where(live[:, None, None], weight_tiles.reshape(CAP, TILE, TILE), 0)
    packed = tiles.reshape(PAIRS, 2, TILE, TILE).transpose(0, 3, 1, 2).reshape(PACK, PAIR)
    ids = tile_ids.reshape(1, CAP)
    block = 2 * lax.axis_index("y") + lax.axis_index("core")
    d = ids // PER_COL
    unit = d // SUB * (NZ * SUB) + block * SUB + d % SUB
    meta = jnp.pad(unit, ((0, META - 1), (0, PAIR - CAP))) + jnp.pad(
        ids % PER_COL, ((0, META - 1), (F_LANE, PAIR - F_LANE - CAP))
    )
    sent = jnp.concatenate([packed, meta.astype(jnp.bfloat16)], axis=0)
    wide = jnp.broadcast_to(sent[None], (NY, ROWS, PAIR))
    w_own = lax.all_to_all(wide, "y", split_axis=0, concat_axis=0, tiled=True)

    x_mine = activations.T.reshape(1, SHARD // 16, 16, TOK)
    x0 = lax.all_gather(x_mine, "z", axis=0, tiled=True).reshape(COL_ROWS, TOK)
    lower, upper = x0[:CUT], x0[CUT:]
    near, far = trade(1), trade(3)
    x1a = lax.ppermute(lower, "x", near)
    x3b = lax.ppermute(upper, "x", far)
    x1b = lax.ppermute(upper, "x", near)
    x3a = lax.ppermute(lower, "x", far)
    x2a = lax.ppermute(x1a, "x", far)
    x2b = lax.ppermute(x3b, "x", near)
    w_other = lax.ppermute(w_own, "core", SWAP)

    table0, table1 = (
        jnp.sum(w[:, PACK:, :].astype(jnp.float32), axis=1).astype(jnp.int32) for w in (w_own, w_other)
    )
    here = lax.axis_index("x").astype(jnp.int32).reshape(1)
    x, tiles0, acc, todo0 = own_step(table0, here, x0, x1a, x1b, x3a, x3b, w_own)
    tiles1, acc, todo1 = other_step(table1, here, x, acc, w_other)
    output, grad, x, theirs = main_step(
        table0, table1, here, todo0, todo1, x, tiles0, tiles1, acc, x2a, x2b, upstream
    )
    arrived = lax.ppermute(theirs, "core", SWAP)
    mine = rest_step(table0, x, grad)
    both = (mine.astype(jnp.float32) + arrived.astype(jnp.float32)).astype(jnp.bfloat16)
    parts = lax.all_to_all(both, "y", split_axis=0, concat_axis=0, tiled=True)
    summed = jnp.sum(parts.astype(jnp.float32), axis=0)
    summed = summed.reshape(PAIRS, TILE, 2, TILE).transpose(0, 2, 3, 1).reshape(CAP, TILE * TILE)
    result = jnp.where(live[:, None], summed, 0.0).astype(jnp.bfloat16)
    return output, result.reshape(1, 1, CAP, TILE * TILE)


def solution(mesh):
    fine = Mesh(mesh.devices.reshape(NZ, NX, NY, 2), ("z", "x", "y", "core"))
    rows, cols = ("z", "x"), ("y", "core")
    return jax.shard_map(
        body,
        mesh=fine,
        in_specs=(
            P(cols, rows),
            P(cols, rows, None, None),
            P(cols, rows, None),
            P(cols, rows),
            P(cols, rows),
        ),
        out_specs=(P(cols, rows), P(cols, rows, None, None)),
        check_vma=False,
    )
```

```python
import jax
import jax.numpy as jnp
from jax import lax
from jax.experimental import pallas as pl
from jax.experimental.pallas import tpu as pltpu
from jax.sharding import Mesh, PartitionSpec as P


TILE = 64
PAIR = 2 * TILE
CAP = 12
PAIRS = CAP // 2
PACK = PAIRS * TILE
META = 16
ROWS = PACK + META
PER_COL = 6
SUB = 3
F_LANE = 16
NZ, NX, NY = 16, 4, 8
SHARD = 192
COL_ROWS = NZ * SHARD
CUT = COL_ROWS // 2
X_ROWS = NX * COL_ROWS
UNITS = COL_ROWS // TILE
GROUP = 8
FF_LOC = 384
TOK = 128


VMEM = pl.BlockSpec(memory_space=pltpu.VMEM)
ANY = pl.BlockSpec(memory_space=pl.ANY)
SMEM = pl.BlockSpec(memory_space=pltpu.SMEM)


def aligned(start, size):
    return pl.ds(pl.multiple_of(start, size), size)


def lanes_below():
    return lax.broadcasted_iota(jnp.int32, (1, PAIR), 1) < TILE


def two(ref, start0, start1):
    return jnp.concatenate([ref[aligned(start0 * TILE, TILE), :], ref[aligned(start1 * TILE, TILE), :]], axis=0)


def slot_grads(table, x, grad_t, dw, b):
    low = lanes_below()
    for m in range(PAIRS):
        s = 2 * m
        cols = two(grad_t, table[b, F_LANE + s], table[b, F_LANE + s + 1])
        rows = two(x, table[b, s], table[b, s + 1])
        prod = lax.dot_general(cols, rows, (((1,), (1,)), ((), ())), preferred_element_type=jnp.float32)
        dw[b, m * TILE : (m + 1) * TILE, :] = jnp.where(low, prod[:TILE], prod[TILE:]).astype(jnp.bfloat16)


def lane_masks():
    low = lanes_below()
    return jnp.where(low, 1.0, 0.0).astype(jnp.bfloat16), jnp.where(low, 0.0, 1.0).astype(jnp.bfloat16)


def list_slots(table, opposite, todo):
    def sort_out(b, n):
        for s in range(CAP):
            todo[0, n] = b * 16 + s
            todo[1, n] = table[b, F_LANE + s]
            ahead = table[b, s] - opposite * UNITS
            n = n + jnp.where((ahead >= 0) & (ahead < UNITS), 1, 0)
        return n

    count = lax.fori_loop(0, NY, sort_out, 0)
    for i in range(GROUP):
        todo[0, count + i] = 0
        todo[1, count + i] = PER_COL
    todo[2, 0] = count


def add_blocks(table, tiles, x, acc):
    first, second = lane_masks()

    def forward(b, carry):
        for m in range(PAIRS):
            s = 2 * m
            tile = tiles[b, m * TILE : (m + 1) * TILE, :]
            prod = jnp.dot(
                jnp.concatenate([tile * first, tile * second], axis=0),
                two(x, table[b, s], table[b, s + 1]),
                preferred_element_type=jnp.float32,
            )
            for p in range(2):
                acc[aligned(table[b, F_LANE + s + p] * TILE, TILE), :] += prod[p * TILE : (p + 1) * TILE]
        return carry

    lax.fori_loop(0, NY, forward, 0, unroll=4)


def add_listed(todo, table, tiles, x, acc):
    first, second = lane_masks()

    def forward(g, carry):
        for i in range(GROUP):
            j = todo[0, g * GROUP + i]
            b, s = j >> 4, j & 15
            m = s >> 1
            tile = tiles[b, aligned(m * TILE, TILE), :]
            prod = jnp.dot(
                tile * jnp.where((s & 1) == 0, first, second),
                two(x, table[b, 2 * m], table[b, 2 * m + 1]),
                preferred_element_type=jnp.float32,
            )
            acc[aligned(todo[1, g * GROUP + i] * TILE, TILE), :] += prod
        return carry

    lax.fori_loop(0, (todo[2, 0] + GROUP - 1) // GROUP, forward, 0)


def own_kernel(table, here, x0, x1a, x1b, x3a, x3b, w, x, tiles, acc, todo, sem):
    opposite = here[0] ^ 2
    x[pl.ds(pl.multiple_of(opposite * COL_ROWS, COL_ROWS), COL_ROWS), :] = jnp.zeros((COL_ROWS, TOK), jnp.bfloat16)

    def part(distance, start, size):
        column = here[0] ^ distance
        return x.at[pl.ds(pl.multiple_of(column * COL_ROWS + start, CUT), size), :]

    moves = [
        (x0, part(0, 0, COL_ROWS)),
        (x1a, part(1, 0, CUT)),
        (x1b, part(1, CUT, CUT)),
        (x3a, part(3, 0, CUT)),
        (x3b, part(3, CUT, CUT)),
        (w, tiles),
    ]
    copies = [pltpu.make_async_copy(a, b, sem.at[i]) for i, (a, b) in enumerate(moves)]
    for c in copies:
        c.start()
    acc[...] = jnp.zeros_like(acc)
    list_slots(table, opposite, todo)
    for c in copies:
        c.wait()
    add_blocks(table, tiles, x, acc)


def main_kernel(
    table0, table1, here, todo, x_in, tiles0, tiles1, acc_in, x2a, x2b, up, out, grad_t, x, dw, acc, sem
):
    base = (here[0] ^ 2) * COL_ROWS
    copies = [
        pltpu.make_async_copy(x2a, x.at[pl.ds(pl.multiple_of(base, CUT), CUT), :], sem.at[0]),
        pltpu.make_async_copy(x2b, x.at[pl.ds(pl.multiple_of(base + CUT, CUT), CUT), :], sem.at[1]),
    ]
    for c in copies:
        c.start()
    acc[...] = acc_in[...]
    for c in copies:
        c.wait()
    add_blocks(table1, tiles1, x, acc)
    add_listed(todo, table0, tiles0, x, acc)
    pre = acc[:FF_LOC].T
    cumul = 0.5 * (1.0 + lax.erf(pre * 0.7071067811865476))
    density = jnp.exp(-0.5 * pre * pre) * 0.3989422804014327
    out[...] = (pre * cumul).astype(jnp.bfloat16)
    grad_t[...] = (up[...].astype(jnp.float32) * (cumul + pre * density)).T.astype(jnp.bfloat16)

    def backward(y, carry):
        slot_grads(table1, x, grad_t, dw, y)
        return carry

    lax.fori_loop(0, NY, backward, 0, unroll=4)


def rest_kernel(table, x, grad_t, dw):
    def backward(y, carry):
        slot_grads(table, x, grad_t, dw, y)
        return carry

    lax.fori_loop(0, NY, backward, 0, unroll=4)


def params(mib):
    return pltpu.CompilerParams(vmem_limit_bytes=mib << 20)


X_SHAPE = jax.ShapeDtypeStruct((X_ROWS, TOK), jnp.bfloat16)
TILES_SHAPE = jax.ShapeDtypeStruct((NY, ROWS, PAIR), jnp.bfloat16)
ACC_SHAPE = jax.ShapeDtypeStruct((FF_LOC + TILE, TOK), jnp.float32)
TODO_SHAPE = jax.ShapeDtypeStruct((3, 128), jnp.int32)


def own_step(table, here, *parts):
    return pl.pallas_call(
        own_kernel,
        out_shape=(X_SHAPE, TILES_SHAPE, ACC_SHAPE, TODO_SHAPE),
        in_specs=[SMEM, SMEM] + [ANY] * 6,
        out_specs=(VMEM, VMEM, VMEM, SMEM),
        scratch_shapes=[pltpu.SemaphoreType.DMA((6,))],
        compiler_params=params(12),
        cost_estimate=pl.CostEstimate(flops=5 * 10**8, bytes_accessed=6 * 10**6, transcendentals=0),
        name="own_step",
    )(table, here, *parts)


def main_step(*operands):
    return pl.pallas_call(
        main_kernel,
        out_shape=(
            jax.ShapeDtypeStruct((TOK, FF_LOC), jnp.bfloat16),
            jax.ShapeDtypeStruct((FF_LOC, TOK), jnp.bfloat16),
            X_SHAPE,
            jax.ShapeDtypeStruct((NY, PACK, PAIR), jnp.bfloat16),
        ),
        in_specs=[SMEM] * 4 + [VMEM] * 4 + [ANY, ANY, VMEM],
        out_specs=(VMEM, VMEM, VMEM, VMEM),
        scratch_shapes=[pltpu.VMEM((FF_LOC + TILE, TOK), jnp.float32), pltpu.SemaphoreType.DMA((2,))],
        input_output_aliases={4: 2},
        compiler_params=params(14),
        cost_estimate=pl.CostEstimate(flops=10**9, bytes_accessed=8 * 10**6, transcendentals=10**5),
        name="main_step",
    )(*operands)


def rest_step(table, x, grad_t):
    return pl.pallas_call(
        rest_kernel,
        out_shape=jax.ShapeDtypeStruct((NY, PACK, PAIR), jnp.bfloat16),
        in_specs=[SMEM, VMEM, VMEM],
        out_specs=VMEM,
        compiler_params=params(12),
        cost_estimate=pl.CostEstimate(flops=10**9, bytes_accessed=4 * 10**6, transcendentals=0),
        name="rest_step",
    )(table, x, grad_t)


def trade(mask):
    return [(i, i ^ mask) for i in range(NX)]


SWAP = [(0, 1), (1, 0)]


def body(activations, weight_tiles, tile_ids, tile_counts, upstream):
    live = jnp.arange(CAP, dtype=jnp.int32) < tile_counts.reshape(())
    tiles = jnp.where(live[:, None, None], weight_tiles.reshape(CAP, TILE, TILE), 0)
    packed = tiles.reshape(PAIRS, 2, TILE, TILE).transpose(0, 3, 1, 2).reshape(PACK, PAIR)
    ids = tile_ids.reshape(1, CAP)
    block = 2 * lax.axis_index("y") + lax.axis_index("core")
    d = ids // PER_COL
    unit = d // SUB * (NZ * SUB) + block * SUB + d % SUB
    meta = jnp.pad(unit, ((0, META - 1), (0, PAIR - CAP))) + jnp.pad(
        ids % PER_COL, ((0, META - 1), (F_LANE, PAIR - F_LANE - CAP))
    )
    sent = jnp.concatenate([packed, meta.astype(jnp.bfloat16)], axis=0)
    wide = jnp.broadcast_to(sent[None], (NY, ROWS, PAIR))
    w_own = lax.all_to_all(wide, "y", split_axis=0, concat_axis=0, tiled=True)

    x_mine = activations.T.reshape(1, SHARD // 16, 16, TOK)
    x0 = lax.all_gather(x_mine, "z", axis=0, tiled=True).reshape(COL_ROWS, TOK)
    lower, upper = x0[:CUT], x0[CUT:]
    near, far = trade(1), trade(3)
    x1a = lax.ppermute(lower, "x", near)
    x3b = lax.ppermute(upper, "x", far)
    x1b = lax.ppermute(upper, "x", near)
    x3a = lax.ppermute(lower, "x", far)
    x2a = lax.ppermute(x1a, "x", far)
    x2b = lax.ppermute(x3b, "x", near)
    w_other = lax.ppermute(w_own, "core", SWAP)

    table0, table1 = (
        jnp.sum(w[:, PACK:, :].astype(jnp.float32), axis=1).astype(jnp.int32) for w in (w_own, w_other)
    )
    here = lax.axis_index("x").astype(jnp.int32).reshape(1)
    x, tiles, acc, todo = own_step(table0, here, x0, x1a, x1b, x3a, x3b, w_own)
    output, grad, x, theirs = main_step(table0, table1, here, todo, x, tiles, w_other, acc, x2a, x2b, upstream)
    arrived = lax.ppermute(theirs, "core", SWAP)
    mine = rest_step(table0, x, grad)
    both = (mine.astype(jnp.float32) + arrived.astype(jnp.float32)).astype(jnp.bfloat16)
    parts = lax.all_to_all(both, "y", split_axis=0, concat_axis=0, tiled=True)
    summed = jnp.sum(parts.astype(jnp.float32), axis=0)
    summed = summed.reshape(PAIRS, TILE, 2, TILE).transpose(0, 2, 3, 1).reshape(CAP, TILE * TILE)
    result = jnp.where(live[:, None], summed, 0.0).astype(jnp.bfloat16)
    return output, result.reshape(1, 1, CAP, TILE * TILE)


def solution(mesh):
    fine = Mesh(mesh.devices.reshape(NZ, NX, NY, 2), ("z", "x", "y", "core"))
    rows, cols = ("z", "x"), ("y", "core")
    return jax.shard_map(
        body,
        mesh=fine,
        in_specs=(
            P(cols, rows),
            P(cols, rows, None, None),
            P(cols, rows, None),
            P(cols, rows),
            P(cols, rows),
        ),
        out_specs=(P(cols, rows), P(cols, rows, None, None)),
        check_vma=False,
    )
```

```python
import jax
import jax.numpy as jnp
from jax import lax
from jax.experimental import pallas as pl
from jax.experimental.pallas import tpu as pltpu
from jax.sharding import Mesh, PartitionSpec as P


TILE = 64
PAIR = 2 * TILE
CAP = 12
PAIRS = CAP // 2
PACK = PAIRS * TILE
META = 16
ROWS = PACK + META
PER_COL = 6
SUB = 3
F_LANE = 16
NZ, NX, NY = 16, 4, 8
SHARD = 192
COL_ROWS = NZ * SHARD
CUT = 7 * SHARD
REST = COL_ROWS - CUT
X_ROWS = NX * COL_ROWS
UNITS = COL_ROWS // TILE
GROUP = 8
FF_LOC = 384
TOK = 128


VMEM = pl.BlockSpec(memory_space=pltpu.VMEM)
ANY = pl.BlockSpec(memory_space=pl.ANY)
SMEM = pl.BlockSpec(memory_space=pltpu.SMEM)


def aligned(start, size):
    return pl.ds(pl.multiple_of(start, size), size)


def lanes_below():
    return lax.broadcasted_iota(jnp.int32, (1, PAIR), 1) < TILE


def two(ref, start0, start1):
    return jnp.concatenate([ref[aligned(start0 * TILE, TILE), :], ref[aligned(start1 * TILE, TILE), :]], axis=0)


def slot_grads(table, x, grad_t, dw, b):
    low = lanes_below()
    for m in range(PAIRS):
        s = 2 * m
        cols = two(grad_t, table[b, F_LANE + s], table[b, F_LANE + s + 1])
        rows = two(x, table[b, s], table[b, s + 1])
        prod = lax.dot_general(cols, rows, (((1,), (1,)), ((), ())), preferred_element_type=jnp.float32)
        dw[b, m * TILE : (m + 1) * TILE, :] = jnp.where(low, prod[:TILE], prod[TILE:]).astype(jnp.bfloat16)


def lane_masks():
    low = lanes_below()
    return jnp.where(low, 1.0, 0.0).astype(jnp.bfloat16), jnp.where(low, 0.0, 1.0).astype(jnp.bfloat16)


def list_slots(table, opposite, todo):
    def sort_out(b, n):
        for s in range(CAP):
            todo[0, n] = b * 16 + s
            todo[1, n] = table[b, F_LANE + s]
            ahead = table[b, s] - opposite * UNITS
            n = n + jnp.where((ahead >= 0) & (ahead < UNITS), 1, 0)
        return n

    count = lax.fori_loop(0, NY, sort_out, 0)
    for i in range(GROUP):
        todo[0, count + i] = 0
        todo[1, count + i] = PER_COL
    todo[2, 0] = count


def add_blocks(table, tiles, x, acc):
    first, second = lane_masks()

    def forward(b, carry):
        for m in range(PAIRS):
            s = 2 * m
            tile = tiles[b, m * TILE : (m + 1) * TILE, :]
            prod = jnp.dot(
                jnp.concatenate([tile * first, tile * second], axis=0),
                two(x, table[b, s], table[b, s + 1]),
                preferred_element_type=jnp.float32,
            )
            for p in range(2):
                acc[aligned(table[b, F_LANE + s + p] * TILE, TILE), :] += prod[p * TILE : (p + 1) * TILE]
        return carry

    lax.fori_loop(0, NY, forward, 0, unroll=4)


def add_listed(todo, table, tiles, x, acc):
    first, second = lane_masks()

    def forward(g, carry):
        for i in range(GROUP):
            j = todo[0, g * GROUP + i]
            b, s = j >> 4, j & 15
            m = s >> 1
            tile = tiles[b, aligned(m * TILE, TILE), :]
            prod = jnp.dot(
                tile * jnp.where((s & 1) == 0, first, second),
                two(x, table[b, 2 * m], table[b, 2 * m + 1]),
                preferred_element_type=jnp.float32,
            )
            acc[aligned(todo[1, g * GROUP + i] * TILE, TILE), :] += prod
        return carry

    lax.fori_loop(0, (todo[2, 0] + GROUP - 1) // GROUP, forward, 0)


def own_kernel(table, here, x0, x1a, x1b, x3a, x3b, w, x, tiles, acc, todo, sem):
    opposite = here[0] ^ 2
    x[pl.ds(pl.multiple_of(opposite * COL_ROWS, COL_ROWS), COL_ROWS), :] = jnp.zeros((COL_ROWS, TOK), jnp.bfloat16)

    def part(distance, start, size):
        column = here[0] ^ distance
        return x.at[pl.ds(pl.multiple_of(column * COL_ROWS + start, TILE), size), :]

    moves = [
        (x0, part(0, 0, COL_ROWS)),
        (x1a, part(1, 0, CUT)),
        (x1b, part(1, CUT, REST)),
        (x3a, part(3, 0, CUT)),
        (x3b, part(3, CUT, REST)),
        (w, tiles),
    ]
    copies = [pltpu.make_async_copy(a, b, sem.at[i]) for i, (a, b) in enumerate(moves)]
    for c in copies:
        c.start()
    acc[...] = jnp.zeros_like(acc)
    list_slots(table, opposite, todo)
    for c in copies:
        c.wait()
    add_blocks(table, tiles, x, acc)


def main_kernel(
    table0, table1, here, todo, x_in, tiles0, tiles1, acc_in, x2a, x2b, up, out, grad_t, x, dw, acc, sem
):
    base = (here[0] ^ 2) * COL_ROWS
    copies = [
        pltpu.make_async_copy(x2a, x.at[pl.ds(pl.multiple_of(base, TILE), CUT), :], sem.at[0]),
        pltpu.make_async_copy(x2b, x.at[pl.ds(pl.multiple_of(base + CUT, TILE), REST), :], sem.at[1]),
    ]
    for c in copies:
        c.start()
    acc[...] = acc_in[...]
    for c in copies:
        c.wait()
    add_blocks(table1, tiles1, x, acc)
    add_listed(todo, table0, tiles0, x, acc)
    pre = acc[:FF_LOC].T
    cumul = 0.5 * (1.0 + lax.erf(pre * 0.7071067811865476))
    density = jnp.exp(-0.5 * pre * pre) * 0.3989422804014327
    out[...] = (pre * cumul).astype(jnp.bfloat16)
    grad_t[...] = (up[...].astype(jnp.float32) * (cumul + pre * density)).T.astype(jnp.bfloat16)

    def backward(y, carry):
        slot_grads(table1, x, grad_t, dw, y)
        return carry

    lax.fori_loop(0, NY, backward, 0, unroll=4)


def rest_kernel(table, x, grad_t, dw):
    def backward(y, carry):
        slot_grads(table, x, grad_t, dw, y)
        return carry

    lax.fori_loop(0, NY, backward, 0, unroll=4)


def params(mib):
    return pltpu.CompilerParams(vmem_limit_bytes=mib << 20)


X_SHAPE = jax.ShapeDtypeStruct((X_ROWS, TOK), jnp.bfloat16)
TILES_SHAPE = jax.ShapeDtypeStruct((NY, ROWS, PAIR), jnp.bfloat16)
ACC_SHAPE = jax.ShapeDtypeStruct((FF_LOC + TILE, TOK), jnp.float32)
TODO_SHAPE = jax.ShapeDtypeStruct((3, 128), jnp.int32)


def own_step(table, here, *parts):
    return pl.pallas_call(
        own_kernel,
        out_shape=(X_SHAPE, TILES_SHAPE, ACC_SHAPE, TODO_SHAPE),
        in_specs=[SMEM, SMEM] + [ANY] * 6,
        out_specs=(VMEM, VMEM, VMEM, SMEM),
        scratch_shapes=[pltpu.SemaphoreType.DMA((6,))],
        compiler_params=params(12),
        cost_estimate=pl.CostEstimate(flops=5 * 10**8, bytes_accessed=6 * 10**6, transcendentals=0),
        name="own_step",
    )(table, here, *parts)


def main_step(*operands):
    return pl.pallas_call(
        main_kernel,
        out_shape=(
            jax.ShapeDtypeStruct((TOK, FF_LOC), jnp.bfloat16),
            jax.ShapeDtypeStruct((FF_LOC, TOK), jnp.bfloat16),
            X_SHAPE,
            jax.ShapeDtypeStruct((NY, PACK, PAIR), jnp.bfloat16),
        ),
        in_specs=[SMEM] * 4 + [VMEM] * 4 + [ANY, ANY, VMEM],
        out_specs=(VMEM, VMEM, VMEM, VMEM),
        scratch_shapes=[pltpu.VMEM((FF_LOC + TILE, TOK), jnp.float32), pltpu.SemaphoreType.DMA((2,))],
        input_output_aliases={4: 2},
        compiler_params=params(14),
        cost_estimate=pl.CostEstimate(flops=10**9, bytes_accessed=8 * 10**6, transcendentals=10**5),
        name="main_step",
    )(*operands)


def rest_step(table, x, grad_t):
    return pl.pallas_call(
        rest_kernel,
        out_shape=jax.ShapeDtypeStruct((NY, PACK, PAIR), jnp.bfloat16),
        in_specs=[SMEM, VMEM, VMEM],
        out_specs=VMEM,
        compiler_params=params(12),
        cost_estimate=pl.CostEstimate(flops=10**9, bytes_accessed=4 * 10**6, transcendentals=0),
        name="rest_step",
    )(table, x, grad_t)


def trade(mask):
    return [(i, i ^ mask) for i in range(NX)]


SWAP = [(0, 1), (1, 0)]


def body(activations, weight_tiles, tile_ids, tile_counts, upstream):
    live = jnp.arange(CAP, dtype=jnp.int32) < tile_counts.reshape(())
    tiles = jnp.where(live[:, None, None], weight_tiles.reshape(CAP, TILE, TILE), 0)
    packed = tiles.reshape(PAIRS, 2, TILE, TILE).transpose(0, 3, 1, 2).reshape(PACK, PAIR)
    ids = tile_ids.reshape(1, CAP)
    block = 2 * lax.axis_index("y") + lax.axis_index("core")
    d = ids // PER_COL
    unit = d // SUB * (NZ * SUB) + block * SUB + d % SUB
    meta = jnp.pad(unit, ((0, META - 1), (0, PAIR - CAP))) + jnp.pad(
        ids % PER_COL, ((0, META - 1), (F_LANE, PAIR - F_LANE - CAP))
    )
    sent = jnp.concatenate([packed, meta.astype(jnp.bfloat16)], axis=0)
    wide = jnp.broadcast_to(sent[None], (NY, ROWS, PAIR))
    w_own = lax.all_to_all(wide, "y", split_axis=0, concat_axis=0, tiled=True)

    x_mine = activations.T.reshape(1, SHARD // 16, 16, TOK)
    x0 = lax.all_gather(x_mine, "z", axis=0, tiled=True).reshape(COL_ROWS, TOK)
    lower = x0[:CUT]
    upper = lax.optimization_barrier(x0)[CUT:]
    near, far = trade(1), trade(3)
    x1a = lax.ppermute(lower, "x", near)
    x3b = lax.ppermute(upper, "x", far)
    x1b = lax.ppermute(upper, "x", near)
    x3a = lax.ppermute(lower, "x", far)
    x2a = lax.ppermute(x1a, "x", far)
    x2b = lax.ppermute(x3b, "x", near)
    w_other = lax.ppermute(w_own, "core", SWAP)

    table0, table1 = (
        jnp.sum(w[:, PACK:, :].astype(jnp.float32), axis=1).astype(jnp.int32) for w in (w_own, w_other)
    )
    here = lax.axis_index("x").astype(jnp.int32).reshape(1)
    x, tiles, acc, todo = own_step(table0, here, x0, x1a, x1b, x3a, x3b, w_own)
    output, grad, x, theirs = main_step(table0, table1, here, todo, x, tiles, w_other, acc, x2a, x2b, upstream)
    arrived = lax.ppermute(theirs, "core", SWAP)
    mine = rest_step(table0, x, grad)
    both = (mine.astype(jnp.float32) + arrived.astype(jnp.float32)).astype(jnp.bfloat16)
    parts = lax.all_to_all(both, "y", split_axis=0, concat_axis=0, tiled=True)
    summed = jnp.sum(parts.astype(jnp.float32), axis=0)
    summed = summed.reshape(PAIRS, TILE, 2, TILE).transpose(0, 2, 3, 1).reshape(CAP, TILE * TILE)
    result = jnp.where(live[:, None], summed, 0.0).astype(jnp.bfloat16)
    return output, result.reshape(1, 1, CAP, TILE * TILE)


def solution(mesh):
    fine = Mesh(mesh.devices.reshape(NZ, NX, NY, 2), ("z", "x", "y", "core"))
    rows, cols = ("z", "x"), ("y", "core")
    return jax.shard_map(
        body,
        mesh=fine,
        in_specs=(
            P(cols, rows),
            P(cols, rows, None, None),
            P(cols, rows, None),
            P(cols, rows),
            P(cols, rows),
        ),
        out_specs=(P(cols, rows), P(cols, rows, None, None)),
        check_vma=False,
    )
```
